32 devices in a mesh: chan: 16 (over z, x, core), tm: 2 (over y).
Axes of the slice: x: 2, y: 2, z: 4, core: 2. Of those that a mesh axis runs over, the one named last changes fastest.
Arguments:
- traces: bfloat16 [512, 4, 2048], P('chan', None, 'tm'), may hold values from -40 to 40
- delays: int32 [128, 512], P(None, 'chan'), may hold values from 0 to 1023
- offsets: int32 [4], P('tm'), may hold values from 0 to 2047
Outputs:
- brightness: float32 [4, 128, 256], P('tm', 'chan')
The draws below stay inside these ranges and needn't reach their ends.
All inputs are finite; a program needn't handle non-finite values.
Results may differ from the reference program's by a relative error of at most 0.0048.
Values may be sent and summed in bfloat16 or wider, within the bound.
A program may use at most 64 MiB of HBM per device.

```python
import math
import jax
import jax.numpy as jnp
from jax import lax

CH_DEV = 32
WINDOWS = 4
NODES_DEV = 8
SAMPLES = 2048
BAND = 512
FB = 128
TB = 256
BAND_LO = 128
DEC = 8
CHANNELS = 512
NODES = 128
N_CHAN = 16


def draw_traces(key, part):
    keys = jax.random.split(jax.random.fold_in(key, 17), 3)
    block_len = SAMPLES // 8
    channel_scale = jnp.exp(jax.random.uniform(keys[0], (CHANNELS, 1, 1, 1), jnp.float32) * math.log(10.0))
    block_scale = jnp.exp(jax.random.uniform(keys[1], (CHANNELS, WINDOWS, 8, 1), jnp.float32) * math.log(10.0))
    noise = jnp.clip(jax.random.normal(keys[2], (CHANNELS, WINDOWS, 8, block_len), jnp.float32), -4.0, 4.0)
    values = noise * block_scale * channel_scale / 10.0
    return values.reshape(CHANNELS, WINDOWS, SAMPLES).astype(jnp.bfloat16)


def set_ends(result, own_key, low, high):
    extent = result.shape
    index_at = [jax.random.randint(jax.random.fold_in(own_key, axis), (), 0, extent[axis]) for axis in range(len(extent))]
    result = result.at[tuple(index_at)].set(low)
    longest = extent.index(max(extent))
    index_at[longest] = (index_at[longest] + 1) % extent[longest]
    return result.at[tuple(index_at)].set(high)


def setup_inputs(seed: int = 0) -> dict:
    splits = jax.random.split(jax.random.key(seed), 4)
    return {
        "traces": draw_traces(jax.random.fold_in(splits[3], 71), 0),
        "delays": set_ends(jax.random.randint(splits[1], (NODES, CHANNELS), 0, SAMPLES // 2), jax.random.fold_in(splits[1], 1), 0, (SAMPLES // 2) - 1).astype(jnp.int32),
        "offsets": set_ends(jax.random.randint(splits[2], (WINDOWS,), 0, SAMPLES), jax.random.fold_in(splits[2], 1), 0, SAMPLES - 1).astype(jnp.int32),
    }


epsilon = 1e-06
full_turn = 2.0 * math.pi

def angle_grid(first_ids, second_ids):
    product = first_ids[:, None] * second_ids[None, :] % SAMPLES
    return product.astype(jnp.float32) * (full_turn / SAMPLES)

def reference(traces, delays, offsets):
    sample_ids = jnp.arange(SAMPLES, dtype=jnp.int32)
    band_bins = BAND_LO + jnp.arange(BAND, dtype=jnp.int32)
    taper = jnp.sin(jnp.pi * (jnp.arange(BAND, dtype=jnp.float32) + 0.5) / BAND) ** 2
    forward_angles = angle_grid(sample_ids, band_bins)
    forward = jnp.concatenate([jnp.cos(forward_angles), -jnp.sin(forward_angles)], axis=1).astype(jnp.bfloat16)
    back_angles = angle_grid(band_bins, sample_ids)
    weight = (2.0 * taper / SAMPLES)[:, None]
    upper = jnp.concatenate([weight * jnp.cos(back_angles), weight * jnp.sin(back_angles)], axis=1)
    lower = jnp.concatenate([-weight * jnp.sin(back_angles), weight * jnp.cos(back_angles)], axis=1)
    inverse = jnp.concatenate([upper, lower], axis=0).astype(jnp.bfloat16)
    env_bins = 1 + jnp.arange(FB, dtype=jnp.int32)
    env_angles = angle_grid(sample_ids, env_bins)
    envelope_table = jnp.concatenate([jnp.cos(env_angles), -jnp.sin(env_angles)], axis=1).astype(jnp.bfloat16)

    def process(block_traces):
        trace_rows = block_traces.reshape(CH_DEV * WINDOWS, SAMPLES)
        spectrum = jnp.dot(trace_rows, forward, preferred_element_type=jnp.float32).astype(jnp.bfloat16)
        analytic = jnp.dot(spectrum, inverse, preferred_element_type=jnp.float32)
        real_part = analytic[:, :SAMPLES]
        imag_part = analytic[:, SAMPLES:]
        energy = real_part * real_part + imag_part * imag_part
        energy_sum = lax.optimization_barrier(jnp.sum(energy, axis=1))
        envelope_spectrum = jnp.dot(energy.astype(jnp.bfloat16), envelope_table, preferred_element_type=jnp.float32)
        factor = 1.0 / (math.sqrt(SAMPLES) * (energy_sum / SAMPLES + epsilon))
        normalized = (envelope_spectrum * factor[:, None]).astype(jnp.bfloat16)
        return normalized.reshape(CH_DEV, WINDOWS, 2 * FB)
    normalized = lax.map(process, traces.reshape(N_CHAN, CH_DEV, WINDOWS, SAMPLES))
    normalized = normalized.reshape(CHANNELS, WINDOWS, 2 * FB)
    e_real = normalized[:, :, :FB]
    e_imag = normalized[:, :, FB:]
    real_block = jnp.concatenate([e_real, -e_imag], axis=0)
    imag_block = jnp.concatenate([e_imag, e_real], axis=0)
    spectra_pair = jnp.concatenate([real_block, imag_block], axis=1).astype(jnp.float32)

    def stack_block(delay_rows):
        product = delay_rows[:, :, None] * env_bins[None, None, :] % SAMPLES
        angles = product.astype(jnp.float32) * (full_turn / SAMPLES)
        phase = jnp.concatenate([jnp.cos(angles), jnp.sin(angles)], axis=1).astype(jnp.bfloat16)
        return jnp.einsum('ncf,cwf->nwf', phase.astype(jnp.float32), spectra_pair)
    stacks = lax.map(stack_block, delays.reshape(N_CHAN, NODES_DEV, CHANNELS))
    stacks = stacks.reshape(NODES, 2, WINDOWS, FB)
    out_times = offsets[:, None] + DEC * jnp.arange(TB, dtype=jnp.int32)[None, :]
    product = env_bins[None, :, None] * out_times[:, None, :] % SAMPLES
    out_angles = product.astype(jnp.float32) * (full_turn / SAMPLES)
    scale = 1.0 / math.sqrt(FB * CHANNELS)
    bright = jnp.einsum('nwf,wfk->wnk', stacks[:, 0], jnp.cos(out_angles), precision=lax.Precision.HIGHEST)
    bright = bright - jnp.einsum('nwf,wfk->wnk', stacks[:, 1], jnp.sin(out_angles), precision=lax.Precision.HIGHEST)
    return bright * scale
```

```python
import functools
import math

import jax
import jax.numpy as jnp
from jax import lax
from jax.experimental import pallas as pl
from jax.experimental.pallas import tpu as pltpu
from jax.sharding import PartitionSpec as P

SAMPLES = 2048
BAND = 512
FB = 128
TB = 256
BAND_LO = 128
DEC = 8
PAIR = 2
CHUNKS = 4

RADIX = 8
SPAN = SAMPLES // RADIX
BINS = BAND // RADIX
TIMES = SAMPLES // 2
FOLD = TIMES // 2
INNER = TIMES // RADIX
HALF_FB = FB // 2

epsilon = 1e-06
full_turn = 2.0 * math.pi
root_half = math.sqrt(0.5)
MESH = pl.DeviceIdType.MESH


COS_TURN = (
    0.9999999890590201, -19.739204499453688, 64.93911745988827, -85.45013953077586,
    60.16763095018129, -25.96759924584206, 6.528658157862129,
)
SIN_TURN = (
    6.283185302511498, -41.341700405316736, 81.60513138576982, -76.70301535347629,
    42.02592698341473, -14.899846660399582, 3.2381375010236435,
)


def cos_sin(turns):
    x = turns - jnp.round(turns)
    y = x * x
    c, s = COS_TURN[-1], SIN_TURN[-1]
    for c_next, s_next in zip(COS_TURN[-2::-1], SIN_TURN[-2::-1]):
        c = c * y + c_next
        s = s * y + s_next
    return c, s * x


def float_iota(shape, axis):
    return lax.broadcasted_iota(jnp.int32, shape, axis).astype(jnp.float32)


def bit_of(value, at):
    return lax.rem(value // (1 << at), 2)


def flip(value, at):
    return value + (1 - 2 * bit_of(value, at)) * (1 << at)


def split(value):
    high = value.astype(jnp.bfloat16)
    return high, (value - high.astype(jnp.float32)).astype(jnp.bfloat16)


def env_bins(axis):
    shape = (1, FB) if axis else (FB, 1)
    lane = lax.broadcasted_iota(jnp.int32, shape, axis)
    return jnp.where(lane < HALF_FB, 2 * lane + 2, 2 * lane - (FB - 1)).astype(jnp.float32)


def inverse_four(values):
    (ar, ai), (br, bi), (cr, ci), (dr, di) = values
    sr, si, er, ei = ar + cr, ai + ci, ar - cr, ai - ci
    tr, ti, fr, fi = br + dr, bi + di, br - dr, bi - di
    return [(sr + tr, si + ti), (er - fi, ei + fr), (sr - tr, si - ti), (er + fi, ei - fr)]


def kernel(
    n_chan, x_hbm, d_hbm, off_hbm, out_ref,
    d_ref, own, other, fwd, inv, env, fwd_c, fwd_s, inv_c, inv_s, gain, phase_c, phase_s,
    nodes_d, turn_tab, turn_row, e_tab, acc, send_buf, recv_buf,
    off_ref, off_sem, d_sem, x_in, x_send, x_recv, send_sem, recv_sem, round_sem,
):
    chans, kept, half = own.shape
    group = chans // CHUNKS
    rows = kept * group
    nodes = d_hbm.shape[1]
    node_rows = nodes // n_chan
    me = lax.axis_index("chan")
    tm = lax.axis_index("tm")
    partner = 1 - tm
    unit = 1.0 / SAMPLES

    rounds = n_chan.bit_length() - 1
    barrier = pltpu.get_barrier_semaphore()
    pl.semaphore_signal(barrier, inc=1, device_id={"tm": partner}, device_id_type=MESH)
    for r in range(rounds):
        pl.semaphore_signal(barrier, inc=1, device_id={"chan": flip(me, r)}, device_id_type=MESH)

    offsets_in = pltpu.make_async_copy(off_hbm, off_ref, off_sem)
    delays_in = pltpu.make_async_copy(d_hbm, d_ref, d_sem)
    own_in = pltpu.make_async_copy(
        x_hbm.at[:, pl.ds(pl.multiple_of(tm * kept, kept), kept)], own, x_in
    )
    delays_in.start()
    offsets_in.start()
    own_in.start()

    def tell(r):
        if r < rounds:
            pl.semaphore_signal(round_sem.at[r], inc=1, device_id={"chan": flip(me, r)}, device_id_type=MESH)

    def hear(r):
        if r < rounds:
            pl.semaphore_wait(round_sem.at[r], 1)
            tell(r + 1)

    def exchange(first, count, at):
        return pltpu.make_async_remote_copy(
            src_ref=x_hbm.at[pl.ds(first, count), pl.ds(pl.multiple_of(partner * kept, kept), kept)],
            dst_ref=other.at[pl.ds(first, count)],
            send_sem=x_send,
            recv_sem=x_recv.at[at],
            device_id={"tm": partner},
            device_id_type=MESH,
        )

    pl.semaphore_wait(barrier, rounds + 1)
    for g in range(CHUNKS):
        exchange(g * group, group, g).start()
    tell(0)

    late = jnp.where(lax.broadcasted_iota(jnp.int32, (1, SPAN), 1) * 0 + tm == 1, -1.0, 1.0)
    residue = lax.broadcasted_iota(jnp.int32, (RADIX, SPAN), 0)
    c, s = cos_sin(residue.astype(jnp.float32) * float_iota((RADIX, SPAN), 1) * unit)
    sign = jnp.where((residue & 1) == 1, late, 1.0)
    fwd_c[...] = c * sign
    fwd_s[...] = s * sign
    inv_c[...], inv_s[...] = cos_sin(float_iota((RADIX, INNER), 0) * float_iota((RADIX, INNER), 1) * (1.0 / TIMES))
    lane = lax.broadcasted_iota(jnp.int32, (1, 2 * BINS), 1)
    quarter = jnp.where(lane < BINS, 0.0, 0.25)
    place = jnp.where(lane < BINS, lane, lane - BINS).astype(jnp.float32)
    _, s = cos_sin((RADIX * place + float_iota((RADIX, 2 * BINS), 0) + 0.5) * (0.5 / BAND))
    gain[...] = s * s * (2.0 / SAMPLES)

    def forward_table(at):
        first = pl.multiple_of(at * 32, 32)
        spot = float_iota((32, 2 * BINS), 0) + first.astype(jnp.float32)
        c, s = cos_sin(spot * ((place + BAND_LO // RADIX) * (1.0 / SPAN)) + quarter)
        for value, base in ((c, 0), (s, SPAN)):
            high, low = split(value)
            fwd[pl.ds(pl.multiple_of(base + first, 32), 32), : 2 * BINS] = high
            fwd[pl.ds(pl.multiple_of(base + first, 32), 32), 2 * BINS :] = low

    pl.loop(0, SPAN // 32)(forward_table)

    row = lax.broadcasted_iota(jnp.int32, (2 * BINS, 1), 0)
    row_quarter = jnp.where(row < BINS, 0.0, 0.25)
    row_place = jnp.where(row < BINS, row, row - BINS).astype(jnp.float32)
    c, s = cos_sin(row_place * (float_iota((1, INNER), 1) * (1.0 / INNER)) + row_quarter)
    for base in (0, 2 * BINS):
        inv[base : base + 2 * BINS, :INNER] = c.astype(jnp.bfloat16)
        inv[base : base + 2 * BINS, INNER:] = s.astype(jnp.bfloat16)

    env_lane = lax.broadcasted_iota(jnp.int32, (1, FB), 1)
    env_quarter = jnp.where(env_lane < HALF_FB, 0.0, 0.25)
    env_place = jnp.where(env_lane < HALF_FB, env_lane, env_lane - HALF_FB).astype(jnp.float32)
    for odd in range(2):
        freq = (2.0 * env_place + (1.0 if odd else 2.0)) * (1.0 / TIMES)
        base_c, base_s = cos_sin(float_iota((32, FB), 0) * freq + env_quarter)
        lead_c, lead_s = cos_sin(float_iota((FOLD // 32, FB), 0) * (freq * 32.0))
        for a in range(FOLD // 32):
            value = lead_c[a : a + 1] * base_c - lead_s[a : a + 1] * base_s
            env[odd, a * 32 : (a + 1) * 32, :] = value.astype(jnp.bfloat16)

    hear(0)

    delays_in.wait()
    nodes_d[...] = (d_ref[...].astype(jnp.float32) * unit).T
    block = PAIR * node_rows
    bins = env_bins(1)
    pairs = n_chan // PAIR

    def phases(step):
        at = pl.ds(pl.multiple_of(step * block, block), block)
        delay = nodes_d[at, :]
        for ch in range(chans):
            c, s = cos_sin(delay[:, ch : ch + 1] * bins)
            phase_c[ch, at, :] = c
            phase_s[ch, at, :] = s
        acc[step] = jnp.zeros(acc.shape[1:], jnp.float32)

    pl.loop(0, pairs // 2)(phases)
    hear(1)
    pl.loop(pairs // 2, pairs)(phases)
    hear(2)

    turns = env_bins(0)
    c, s = cos_sin(turns * (float_iota((1, TB), 1) * (DEC * unit)))
    turn_tab[:FB, :] = c
    turn_tab[FB:, :] = -s
    offsets_in.wait()
    for w in range(kept):
        shift = off_ref[w].astype(jnp.float32) * unit
        turn_row[w, :, :FB], turn_row[w, :, FB:] = cos_sin(bins * shift)

    for r in range(3, rounds):
        hear(r)
    own_in.wait()

    def envelope(g):
        at = pl.ds(pl.multiple_of(g * group, group), group)
        mine = own[at].reshape(rows, half).astype(jnp.float32)
        theirs = other[at].reshape(rows, half).astype(jnp.float32)
        a, b = [], []
        for q in range(RADIX // 2):
            cols = slice(q * SPAN, (q + 1) * SPAN)
            a.append(mine[:, cols] + theirs[:, cols])
            b.append(mine[:, cols] - theirs[:, cols])
        s02, d02, s13, d13 = a[0] + a[2], a[0] - a[2], a[1] + a[3], a[1] - a[3]
        t, u = (b[1] - b[3]) * root_half, (b[1] + b[3]) * root_half
        one = (b[0] + t, -(u + b[2]))
        three = (b[0] - t, b[2] - u)
        parts = [
            (s02 + s13, None), one, (d02, -d13), three,
            (s02 - s13, None), (three[0], -three[1]), (d02, d13), (one[0], -one[1]),
        ]
        stacked = []
        for r, (re, im) in enumerate(parts):
            if r == 0:
                zr, zi = re, jnp.zeros_like(re)
            else:
                c, s = fwd_c[r : r + 1, :], fwd_s[r : r + 1, :]
                if im is None:
                    zr, zi = re * c, -(re * s)
                else:
                    zr, zi = re * c + im * s, im * c - re * s
            stacked.append(jnp.concatenate([zr, zi], axis=1).astype(jnp.bfloat16))
        spectrum = jnp.dot(
            jnp.concatenate(stacked, axis=0), fwd[...], preferred_element_type=jnp.float32
        )
        spectrum = spectrum[:, : 2 * BINS] + spectrum[:, 2 * BINS :]
        tapered = []
        for r in range(RADIX):
            high, low = split(spectrum[r * rows : (r + 1) * rows] * gain[r : r + 1, :])
            tapered.append(jnp.concatenate([high, low], axis=1))
        inner = jnp.dot(jnp.concatenate(tapered, axis=0), inv[...], preferred_element_type=jnp.float32)
        turned = []
        for r in range(RADIX):
            re = inner[r * rows : (r + 1) * rows, :INNER]
            im = inner[r * rows : (r + 1) * rows, INNER:]
            if r:
                c, s = inv_c[r : r + 1, :], inv_s[r : r + 1, :]
                re, im = re * c - im * s, re * s + im * c
            turned.append((re, im))
        evens, odds = inverse_four(turned[0::2]), inverse_four(turned[1::2])
        same, cross = [], []
        for q in range(RADIX // 2):
            (er, ei), (fr, fi) = evens[q], odds[q]
            same.append((er * er + ei * ei) + (fr * fr + fi * fi))
            if q == 0:
                both = 2.0 * (er * fr + ei * fi)
            elif q == 1:
                both = (2.0 * root_half) * (er * (fr - fi) + ei * (fr + fi))
            elif q == 2:
                both = 2.0 * (ei * fr - er * fi)
            else:
                both = (2.0 * root_half) * (ei * (fr - fi) - er * (fr + fi))
            cross.append(both)
        total = jnp.sum((same[0] + same[1]) + (same[2] + same[3]), axis=1, keepdims=True)
        even = jnp.dot(
            jnp.concatenate(same, axis=1).astype(jnp.bfloat16), env[0], preferred_element_type=jnp.float32
        )
        odd = jnp.dot(
            jnp.concatenate(cross, axis=1).astype(jnp.bfloat16), env[1], preferred_element_type=jnp.float32
        )
        factor = 4.0 / (math.sqrt(SAMPLES) * (total * (4.0 / SAMPLES) + epsilon))
        even, odd = even * factor, odd * factor
        lower = lax.broadcasted_iota(jnp.int32, (1, FB), 1) < HALF_FB
        e_tab[:, :FB] = jnp.where(lower, even, pltpu.roll(odd, HALF_FB, 1))
        e_tab[:, FB:] = jnp.where(lower, pltpu.roll(even, HALF_FB, 1), odd)

    def outgoing(dest):
        return pltpu.make_async_remote_copy(
            src_ref=send_buf.at[dest],
            dst_ref=recv_buf.at[me],
            send_sem=send_sem,
            recv_sem=recv_sem.at[me],
            device_id={"chan": dest},
            device_id_type=MESH,
        )

    upper = (me // PAIR) // (pairs // 2)

    def pair_at(step):
        return upper * step + (1 - upper) * (pairs - 1 - step)

    def send_pair(step):
        for side in range(PAIR):
            dest = pair_at(step) * PAIR + side

            @pl.when(dest != me)
            def _():
                outgoing(dest).start()

    def stack_up(g, pair):
        at = pl.ds(pl.multiple_of(pair * block, block), block)
        sums = [[acc[pair, p * kept + w] for w in range(kept)] for p in range(2)]
        for ch in range(group):
            pc = phase_c[g * group + ch, at, :]
            ps = phase_s[g * group + ch, at, :]
            for w in range(kept):
                r = kept * ch + w
                er, ei = e_tab[r : r + 1, :FB], e_tab[r : r + 1, FB:]
                sums[0][w] = sums[0][w] + (pc * er - ps * ei)
                sums[1][w] = sums[1][w] + (pc * ei + ps * er)
        return sums

    @pl.loop(0, CHUNKS)
    def _(g):
        exchange(g * group, group, g).wait_recv()
        envelope(g)

        @pl.when(g < CHUNKS - 1)
        def _():
            @pl.loop(0, pairs)
            def _(pair):
                sums = stack_up(g, pair)
                for p in range(2):
                    for w in range(kept):
                        acc[pair, p * kept + w] = sums[p][w]

        @pl.when(g == CHUNKS - 1)
        def _():
            @pl.loop(0, pairs)
            def _(step):
                pair = pair_at(step)
                sums = stack_up(g, pair)
                for side in range(PAIR):
                    part = slice(side * node_rows, (side + 1) * node_rows)
                    packed = jnp.concatenate([sums[p][w][part] for p in range(2) for w in range(kept)], axis=0)
                    send_buf[pair * PAIR + side] = packed.astype(jnp.bfloat16)

                @pl.when(step > 0)
                def _():
                    send_pair(step - 1)

    send_pair(pairs - 1)

    def incoming(source):
        return pltpu.make_async_remote_copy(
            src_ref=send_buf.at[source],
            dst_ref=recv_buf.at[source],
            send_sem=send_sem,
            recv_sem=recv_sem.at[source],
            device_id={"chan": source},
            device_id_type=MESH,
        )

    def add_one(step, stack):
        source = lax.rem(me + step, n_chan)
        incoming(source).wait_recv()
        return stack + recv_buf[source].astype(jnp.float32)

    stack = lax.fori_loop(1, n_chan, add_one, send_buf[me].astype(jnp.float32))

    turned = []
    for w in range(kept):
        c, s = turn_row[w, :, :FB], turn_row[w, :, FB:]
        re = stack[w * node_rows : (w + 1) * node_rows]
        im = stack[(kept + w) * node_rows : (kept + w + 1) * node_rows]
        turned.append(jnp.concatenate([re * c - im * s, re * s + im * c], axis=1))
    bright = jnp.dot(
        jnp.concatenate(turned, axis=0), turn_tab[...],
        precision=lax.Precision.HIGHEST, preferred_element_type=jnp.float32,
    )
    scale = 1.0 / math.sqrt(FB * chans * n_chan)
    out_ref[...] = (bright * scale).reshape(kept, node_rows, TB)

    exchange(0, chans, 0).wait_send()
    pltpu.make_async_remote_copy(
        src_ref=send_buf.at[pl.ds(0, n_chan - 1)],
        dst_ref=recv_buf.at[pl.ds(0, n_chan - 1)],
        send_sem=send_sem,
        recv_sem=recv_sem.at[0],
        device_id={"chan": flip(me, 0)},
        device_id_type=MESH,
    ).wait_send()


def solution(mesh):
    n_chan = mesh.shape["chan"]

    def on_device(traces, delays, offsets):
        chans, windows, half = traces.shape
        nodes = delays.shape[0]
        kept = offsets.shape[0]
        node_rows = nodes // n_chan
        block = PAIR * node_rows
        packed_rows = 2 * kept * node_rows
        hbm = pl.BlockSpec(memory_space=pltpu.HBM)
        return pl.pallas_call(
            functools.partial(kernel, n_chan),
            out_shape=jax.ShapeDtypeStruct((kept, node_rows, TB), jnp.float32),
            in_specs=[hbm] * 3,
            out_specs=pl.BlockSpec(memory_space=pltpu.VMEM),
            scratch_shapes=[
                pltpu.VMEM((chans, nodes), jnp.int32),
                pltpu.VMEM((chans, kept, half), jnp.bfloat16),
                pltpu.VMEM((chans, kept, half), jnp.bfloat16),
                pltpu.VMEM((2 * SPAN, 4 * BINS), jnp.bfloat16),
                pltpu.VMEM((4 * BINS, 2 * INNER), jnp.bfloat16),
                pltpu.VMEM((2, FOLD, FB), jnp.bfloat16),
                pltpu.VMEM((RADIX, SPAN), jnp.float32),
                pltpu.VMEM((RADIX, SPAN), jnp.float32),
                pltpu.VMEM((RADIX, INNER), jnp.float32),
                pltpu.VMEM((RADIX, INNER), jnp.float32),
                pltpu.VMEM((RADIX, 2 * BINS), jnp.float32),
                pltpu.VMEM((chans, nodes, FB), jnp.float32),
                pltpu.VMEM((chans, nodes, FB), jnp.float32),
                pltpu.VMEM((nodes, chans), jnp.float32),
                pltpu.VMEM((2 * FB, TB), jnp.float32),
                pltpu.VMEM((kept, 1, 2 * FB), jnp.float32),
                pltpu.VMEM((kept * chans // CHUNKS, 2 * FB), jnp.float32),
                pltpu.VMEM((n_chan // PAIR, 2 * kept, block, FB), jnp.float32),
                pltpu.VMEM((n_chan, packed_rows, FB), jnp.bfloat16),
                pltpu.VMEM((n_chan, packed_rows, FB), jnp.bfloat16),
                pltpu.SMEM((kept,), jnp.int32),
                pltpu.SemaphoreType.DMA,
                pltpu.SemaphoreType.DMA,
                pltpu.SemaphoreType.DMA,
                pltpu.SemaphoreType.DMA,
                pltpu.SemaphoreType.DMA((CHUNKS,)),
                pltpu.SemaphoreType.DMA,
                pltpu.SemaphoreType.DMA((n_chan,)),
                pltpu.SemaphoreType.REGULAR((n_chan.bit_length() - 1,)),
            ],
            compiler_params=pltpu.CompilerParams(
                collective_id=0, has_side_effects=True, vmem_limit_bytes=16 * 1024 * 1024 + 8 * chans * nodes * FB
            ),
        )(*(pltpu.with_memory_space_constraint(a, pltpu.HBM) for a in (traces, delays.T, offsets)))

    placed = (P("chan", None, "tm"), P(None, "chan"), P("tm"))
    return jax.shard_map(
        on_device, mesh=mesh, in_specs=placed, out_specs=P("tm", "chan", None), check_vma=False
    )
```

```python
import functools
import math

import jax
import jax.numpy as jnp
from jax import lax
from jax.experimental import pallas as pl
from jax.experimental.pallas import tpu as pltpu
from jax.sharding import PartitionSpec as P

SAMPLES = 2048
BAND = 512
FB = 128
TB = 256
BAND_LO = 128
DEC = 8
PAIR = 2
CHUNKS = 2
EARLY = 2

RADIX = 8
SPAN = SAMPLES // RADIX
BINS = BAND // RADIX
TIMES = SAMPLES // 2
FOLD = TIMES // 2
INNER = TIMES // RADIX
HALF_FB = FB // 2

epsilon = 1e-06
full_turn = 2.0 * math.pi
root_half = math.sqrt(0.5)
MESH = pl.DeviceIdType.MESH


COS_HALF = (
    1.4142134965650053, -6.978850988237948, 5.73946117066148, -1.8835629871727047, 0.3106981915530425,
)
SIN_HALF = (
    4.442882834149914, -7.30824115454536, 3.6062889582107696, -0.845763596066154, 0.10920575349257165,
)


def cos_sin(turns):
    x = turns - jnp.round(turns)
    y = x * x
    c, s = COS_HALF[-1], SIN_HALF[-1]
    for c_next, s_next in zip(COS_HALF[-2::-1], SIN_HALF[-2::-1]):
        c = c * y + c_next
        s = s * y + s_next
    return c * c - 1.0, s * x * c


def float_iota(shape, axis):
    return lax.broadcasted_iota(jnp.int32, shape, axis).astype(jnp.float32)


def bit_of(value, at):
    return lax.rem(value // (1 << at), 2)


def flip(value, at):
    return value + (1 - 2 * bit_of(value, at)) * (1 << at)


def split(value):
    high = value.astype(jnp.bfloat16)
    return high, (value - high.astype(jnp.float32)).astype(jnp.bfloat16)


def env_bins(axis):
    shape = (1, FB) if axis else (FB, 1)
    lane = lax.broadcasted_iota(jnp.int32, shape, axis)
    return jnp.where(lane < HALF_FB, 2 * lane + 2, 2 * lane - (FB - 1)).astype(jnp.float32)


def inverse_four(values):
    (ar, ai), (br, bi), (cr, ci), (dr, di) = values
    sr, si, er, ei = ar + cr, ai + ci, ar - cr, ai - ci
    tr, ti, fr, fi = br + dr, bi + di, br - dr, bi - di
    return [(sr + tr, si + ti), (er - fi, ei + fr), (sr - tr, si - ti), (er + fi, ei - fr)]


def kernel(
    n_chan, x_hbm, d_hbm, off_hbm, out_ref,
    d_ref, own, other, fwd, inv, env, fwd_c, fwd_s, inv_c, inv_s, gain, phase_c, phase_s,
    nodes_d, turn_tab, turn_row, e_tab, acc, send_buf, recv_buf,
    off_ref, off_sem, d_sem, x_in, x_send, x_recv, send_sem, recv_sem, round_sem,
):
    chans, kept, half = own.shape
    group = chans // CHUNKS
    rows = kept * group
    nodes = d_hbm.shape[1]
    node_rows = nodes // n_chan
    me = lax.axis_index("chan")
    tm = lax.axis_index("tm")
    partner = 1 - tm
    unit = 1.0 / SAMPLES

    rounds = n_chan.bit_length() - 1
    barrier = pltpu.get_barrier_semaphore()
    pl.semaphore_signal(barrier, inc=1, device_id={"tm": partner}, device_id_type=MESH)
    for r in range(rounds):
        pl.semaphore_signal(barrier, inc=1, device_id={"chan": flip(me, r)}, device_id_type=MESH)

    offsets_in = pltpu.make_async_copy(off_hbm, off_ref, off_sem)
    delays_in = pltpu.make_async_copy(d_hbm, d_ref, d_sem)
    own_in = pltpu.make_async_copy(
        x_hbm.at[:, pl.ds(pl.multiple_of(tm * kept, kept), kept)], own, x_in
    )
    delays_in.start()
    offsets_in.start()
    own_in.start()

    def tell(r):
        if r < rounds:
            pl.semaphore_signal(round_sem.at[r], inc=1, device_id={"chan": flip(me, r)}, device_id_type=MESH)

    def hear(r):
        if r < rounds:
            pl.semaphore_wait(round_sem.at[r], 1)
            tell(r + 1)

    def exchange(first, count, at):
        return pltpu.make_async_remote_copy(
            src_ref=x_hbm.at[pl.ds(first, count), pl.ds(pl.multiple_of(partner * kept, kept), kept)],
            dst_ref=other.at[pl.ds(first, count)],
            send_sem=x_send,
            recv_sem=x_recv.at[at],
            device_id={"tm": partner},
            device_id_type=MESH,
        )

    pl.semaphore_wait(barrier, rounds + 1)
    for g in range(CHUNKS):
        exchange(g * group, group, g).start()
    tell(0)

    late = jnp.where(lax.broadcasted_iota(jnp.int32, (1, SPAN), 1) * 0 + tm == 1, -1.0, 1.0)
    residue = lax.broadcasted_iota(jnp.int32, (RADIX, SPAN), 0)
    c, s = cos_sin(residue.astype(jnp.float32) * float_iota((RADIX, SPAN), 1) * unit)
    sign = jnp.where((residue & 1) == 1, late, 1.0)
    fwd_c[...] = c * sign
    fwd_s[...] = s * sign
    inv_c[...], inv_s[...] = cos_sin(float_iota((RADIX, INNER), 0) * float_iota((RADIX, INNER), 1) * (1.0 / TIMES))
    lane = lax.broadcasted_iota(jnp.int32, (1, 2 * BINS), 1)
    quarter = jnp.where(lane < BINS, 0.0, 0.25)
    place = jnp.where(lane < BINS, lane, lane - BINS).astype(jnp.float32)
    _, s = cos_sin((RADIX * place + float_iota((RADIX, 2 * BINS), 0) + 0.5) * (0.5 / BAND))
    gain[...] = s * s * (2.0 / SAMPLES)

    def forward_table(at):
        first = pl.multiple_of(at * 32, 32)
        spot = float_iota((32, 2 * BINS), 0) + first.astype(jnp.float32)
        c, s = cos_sin(spot * ((place + BAND_LO // RADIX) * (1.0 / SPAN)) + quarter)
        for value, base in ((c, 0), (s, SPAN)):
            high, low = split(value)
            fwd[0, pl.ds(pl.multiple_of(base + first, 32), 32), :] = high
            fwd[1, pl.ds(pl.multiple_of(base + first, 32), 32), :] = low

    pl.loop(0, SPAN // 32)(forward_table)

    row = lax.broadcasted_iota(jnp.int32, (2 * BINS, 1), 0)
    row_quarter = jnp.where(row < BINS, 0.0, 0.25)
    row_place = jnp.where(row < BINS, row, row - BINS).astype(jnp.float32)
    c, s = cos_sin(row_place * (float_iota((1, INNER), 1) * (1.0 / INNER)) + row_quarter)
    for base in (0, 2 * BINS):
        inv[0, base : base + 2 * BINS, :] = c.astype(jnp.bfloat16)
        inv[1, base : base + 2 * BINS, :] = s.astype(jnp.bfloat16)

    env_lane = lax.broadcasted_iota(jnp.int32, (1, FB), 1)
    env_quarter = jnp.where(env_lane < HALF_FB, 0.0, 0.25)
    env_place = jnp.where(env_lane < HALF_FB, env_lane, env_lane - HALF_FB).astype(jnp.float32)
    for odd in range(2):
        freq = (2.0 * env_place + (1.0 if odd else 2.0)) * (1.0 / TIMES)
        base_c, base_s = cos_sin(float_iota((32, FB), 0) * freq + env_quarter)
        lead_c, lead_s = cos_sin(float_iota((FOLD // 32, FB), 0) * (freq * 32.0))
        for a in range(FOLD // 32):
            value = lead_c[a : a + 1] * base_c - lead_s[a : a + 1] * base_s
            env[odd, a * 32 : (a + 1) * 32, :] = value.astype(jnp.bfloat16)

    hear(0)

    delays_in.wait()
    nodes_d[...] = (d_ref[...].astype(jnp.float32) * unit).T
    block = PAIR * node_rows
    bins = env_bins(1)
    pairs = n_chan // PAIR

    def phases(step):
        at = pl.ds(pl.multiple_of(step * block, block), block)
        delay = nodes_d[at, :]
        for ch in range(chans):
            c, s = cos_sin(delay[:, ch : ch + 1] * bins)
            phase_c[ch, at, :] = c
            phase_s[ch, at, :] = s

    def two_phases(step):
        phases(2 * step)
        phases(2 * step + 1)

    pl.loop(0, pairs // 4)(two_phases)
    hear(1)
    pl.loop(pairs // 4, pairs // 2)(two_phases)
    hear(2)

    turns = env_bins(0)
    c, s = cos_sin(turns * (float_iota((1, TB), 1) * (DEC * unit)))
    turn_tab[:FB, :] = c
    turn_tab[FB:, :] = -s
    offsets_in.wait()
    for w in range(kept):
        shift = off_ref[w].astype(jnp.float32) * unit
        turn_row[w, :, :FB], turn_row[w, :, FB:] = cos_sin(bins * shift)

    own_in.wait()

    def envelope(g):
        at = pl.ds(pl.multiple_of(g * group, group), group)
        mine = own[at].reshape(rows, half).astype(jnp.float32)
        theirs = other[at].reshape(rows, half).astype(jnp.float32)
        a, b = [], []
        for q in range(RADIX // 2):
            cols = slice(q * SPAN, (q + 1) * SPAN)
            a.append(mine[:, cols] + theirs[:, cols])
            b.append(mine[:, cols] - theirs[:, cols])
        s02, d02, s13, d13 = a[0] + a[2], a[0] - a[2], a[1] + a[3], a[1] - a[3]
        t, u = (b[1] - b[3]) * root_half, (b[1] + b[3]) * root_half
        one = (b[0] + t, -(u + b[2]))
        three = (b[0] - t, b[2] - u)
        parts = [
            (s02 + s13, None), one, (d02, -d13), three,
            (s02 - s13, None), (three[0], -three[1]), (d02, d13), (one[0], -one[1]),
        ]
        stacked = []
        for r, (re, im) in enumerate(parts):
            if r == 0:
                zr, zi = re, jnp.zeros_like(re)
            else:
                c, s = fwd_c[r : r + 1, :], fwd_s[r : r + 1, :]
                if im is None:
                    zr, zi = re * c, -(re * s)
                else:
                    zr, zi = re * c + im * s, im * c - re * s
            stacked.append(jnp.concatenate([zr, zi], axis=1).astype(jnp.bfloat16))
        spectrum = jnp.dot(
            jnp.concatenate(stacked, axis=0), jnp.concatenate([fwd[0], fwd[1]], axis=1), preferred_element_type=jnp.float32
        )
        spectrum = spectrum[:, : 2 * BINS] + spectrum[:, 2 * BINS :]
        tapered = []
        for r in range(RADIX):
            high, low = split(spectrum[r * rows : (r + 1) * rows] * gain[r : r + 1, :])
            tapered.append(jnp.concatenate([high, low], axis=1))
        inner = jnp.dot(jnp.concatenate(tapered, axis=0), jnp.concatenate([inv[0], inv[1]], axis=1), preferred_element_type=jnp.float32)
        turned = []
        for r in range(RADIX):
            re = inner[r * rows : (r + 1) * rows, :INNER]
            im = inner[r * rows : (r + 1) * rows, INNER:]
            if r:
                c, s = inv_c[r : r + 1, :], inv_s[r : r + 1, :]
                re, im = re * c - im * s, re * s + im * c
            turned.append((re, im))
        evens, odds = inverse_four(turned[0::2]), inverse_four(turned[1::2])
        same, cross = [], []
        for q in range(RADIX // 2):
            (er, ei), (fr, fi) = evens[q], odds[q]
            same.append((er * er + ei * ei) + (fr * fr + fi * fi))
            if q == 0:
                both = 2.0 * (er * fr + ei * fi)
            elif q == 1:
                both = (2.0 * root_half) * (er * (fr - fi) + ei * (fr + fi))
            elif q == 2:
                both = 2.0 * (ei * fr - er * fi)
            else:
                both = (2.0 * root_half) * (ei * (fr - fi) - er * (fr + fi))
            cross.append(both)
        total = jnp.sum((same[0] + same[1]) + (same[2] + same[3]), axis=1, keepdims=True)
        even = jnp.dot(
            jnp.concatenate(same, axis=1).astype(jnp.bfloat16), env[0], preferred_element_type=jnp.float32
        )
        odd = jnp.dot(
            jnp.concatenate(cross, axis=1).astype(jnp.bfloat16), env[1], preferred_element_type=jnp.float32
        )
        factor = 4.0 / (math.sqrt(SAMPLES) * (total * (4.0 / SAMPLES) + epsilon))
        even, odd = even * factor, odd * factor
        lower = lax.broadcasted_iota(jnp.int32, (1, FB), 1) < HALF_FB
        e_tab[g, :, :FB] = jnp.where(lower, even, pltpu.roll(odd, HALF_FB, 1))
        e_tab[g, :, FB:] = jnp.where(lower, pltpu.roll(even, HALF_FB, 1), odd)

    def outgoing(dest):
        return pltpu.make_async_remote_copy(
            src_ref=send_buf.at[dest],
            dst_ref=recv_buf.at[me],
            send_sem=send_sem,
            recv_sem=recv_sem.at[me],
            device_id={"chan": dest},
            device_id_type=MESH,
        )

    upper = (me // PAIR) // (pairs // 2)

    def pair_at(step):
        return upper * step + (1 - upper) * (pairs - 1 - step)

    def send_pair(step):
        for side in range(PAIR):
            dest = pair_at(step) * PAIR + side

            @pl.when(dest != me)
            def _():
                outgoing(dest).start()

    def stack_up(g, pair, sums):
        at = pl.ds(pl.multiple_of(pair * block, block), block)
        for ch in range(group):
            pc = phase_c[g * group + ch, at, :]
            ps = phase_s[g * group + ch, at, :]
            for w in range(kept):
                r = kept * ch + w
                er, ei = e_tab[g, r : r + 1, :FB], e_tab[g, r : r + 1, FB:]
                sums[0][w] = sums[0][w] + (pc * er - ps * ei)
                sums[1][w] = sums[1][w] + (pc * ei + ps * er)
        return sums

    def pack(pair, sums):
        for side in range(PAIR):
            part = slice(side * node_rows, (side + 1) * node_rows)
            packed = jnp.concatenate([sums[p][w][part] for p in range(2) for w in range(kept)], axis=0)
            send_buf[pair * PAIR + side] = packed.astype(jnp.bfloat16)

    acc[...] = jnp.zeros_like(acc)

    @pl.loop(0, CHUNKS)
    def _(g):
        exchange(g * group, group, g).wait_recv()
        envelope(g)
        for step in range(EARLY):
            pair = pair_at(step)
            sums = stack_up(g, pair, [[acc[step, p * kept + w] for w in range(kept)] for p in range(2)])
            for p in range(2):
                for w in range(kept):
                    acc[step, p * kept + w] = sums[p][w]

            @pl.when(g == CHUNKS - 1)
            def _():
                pack(pair, sums)
                if step:
                    for r in range(3, rounds):
                        hear(r)
                    send_pair(step - 1)

    @pl.loop(EARLY, pairs)
    def _(step):
        pair = pair_at(step)
        sums = [[jnp.zeros((block, FB), jnp.float32) for _ in range(kept)] for _ in range(2)]
        for g in range(CHUNKS):
            sums = stack_up(g, pair, sums)
        pack(pair, sums)
        send_pair(step - 1)

    send_pair(pairs - 1)

    def incoming(source):
        return pltpu.make_async_remote_copy(
            src_ref=send_buf.at[source],
            dst_ref=recv_buf.at[source],
            send_sem=send_sem,
            recv_sem=recv_sem.at[source],
            device_id={"chan": source},
            device_id_type=MESH,
        )

    def add_one(step, stack):
        source = lax.rem(me + step, n_chan)
        incoming(source).wait_recv()
        return stack + recv_buf[source].astype(jnp.float32)

    stack = lax.fori_loop(1, n_chan, add_one, send_buf[me].astype(jnp.float32))

    turned = []
    for w in range(kept):
        c, s = turn_row[w, :, :FB], turn_row[w, :, FB:]
        re = stack[w * node_rows : (w + 1) * node_rows]
        im = stack[(kept + w) * node_rows : (kept + w + 1) * node_rows]
        turned.append(jnp.concatenate([re * c - im * s, re * s + im * c], axis=1))
    bright = jnp.dot(
        jnp.concatenate(turned, axis=0), turn_tab[...],
        precision=lax.Precision.HIGHEST, preferred_element_type=jnp.float32,
    )
    scale = 1.0 / math.sqrt(FB * chans * n_chan)
    out_ref[...] = (bright * scale).reshape(kept, node_rows, TB)

    exchange(0, chans, 0).wait_send()
    pltpu.make_async_remote_copy(
        src_ref=send_buf.at[pl.ds(0, n_chan - 1)],
        dst_ref=recv_buf.at[pl.ds(0, n_chan - 1)],
        send_sem=send_sem,
        recv_sem=recv_sem.at[0],
        device_id={"chan": flip(me, 0)},
        device_id_type=MESH,
    ).wait_send()


def solution(mesh):
    n_chan = mesh.shape["chan"]

    def on_device(traces, delays, offsets):
        chans, windows, half = traces.shape
        nodes = delays.shape[0]
        kept = offsets.shape[0]
        node_rows = nodes // n_chan
        block = PAIR * node_rows
        packed_rows = 2 * kept * node_rows
        hbm = pl.BlockSpec(memory_space=pltpu.HBM)
        return pl.pallas_call(
            functools.partial(kernel, n_chan),
            out_shape=jax.ShapeDtypeStruct((kept, node_rows, TB), jnp.float32),
            in_specs=[hbm] * 3,
            out_specs=pl.BlockSpec(memory_space=pltpu.VMEM),
            scratch_shapes=[
                pltpu.VMEM((chans, nodes), jnp.int32),
                pltpu.VMEM((chans, kept, half), jnp.bfloat16),
                pltpu.VMEM((chans, kept, half), jnp.bfloat16),
                pltpu.VMEM((2, 2 * SPAN, 2 * BINS), jnp.bfloat16),
                pltpu.VMEM((2, 4 * BINS, INNER), jnp.bfloat16),
                pltpu.VMEM((2, FOLD, FB), jnp.bfloat16),
                pltpu.VMEM((RADIX, SPAN), jnp.float32),
                pltpu.VMEM((RADIX, SPAN), jnp.float32),
                pltpu.VMEM((RADIX, INNER), jnp.float32),
                pltpu.VMEM((RADIX, INNER), jnp.float32),
                pltpu.VMEM((RADIX, 2 * BINS), jnp.float32),
                pltpu.VMEM((chans, nodes, FB), jnp.float32),
                pltpu.VMEM((chans, nodes, FB), jnp.float32),
                pltpu.VMEM((nodes, chans), jnp.float32),
                pltpu.VMEM((2 * FB, TB), jnp.float32),
                pltpu.VMEM((kept, 1, 2 * FB), jnp.float32),
                pltpu.VMEM((CHUNKS, kept * chans // CHUNKS, 2 * FB), jnp.float32),
                pltpu.VMEM((EARLY, 2 * kept, block, FB), jnp.float32),
                pltpu.VMEM((n_chan, packed_rows, FB), jnp.bfloat16),
                pltpu.VMEM((n_chan, packed_rows, FB), jnp.bfloat16),
                pltpu.SMEM((kept,), jnp.int32),
                pltpu.SemaphoreType.DMA,
                pltpu.SemaphoreType.DMA,
                pltpu.SemaphoreType.DMA,
                pltpu.SemaphoreType.DMA,
                pltpu.SemaphoreType.DMA((CHUNKS,)),
                pltpu.SemaphoreType.DMA,
                pltpu.SemaphoreType.DMA((n_chan,)),
                pltpu.SemaphoreType.REGULAR((n_chan.bit_length() - 1,)),
            ],
            compiler_params=pltpu.CompilerParams(
                collective_id=0, has_side_effects=True, vmem_limit_bytes=16 * 1024 * 1024 + 8 * chans * nodes * FB
            ),
        )(*(pltpu.with_memory_space_constraint(a, pltpu.HBM) for a in (traces, delays.T, offsets)))

    placed = (P("chan", None, "tm"), P(None, "chan"), P("tm"))
    return jax.shard_map(
        on_device, mesh=mesh, in_specs=placed, out_specs=P("tm", "chan", None), check_vma=False
    )
```

```python
import functools
import math

import jax
import jax.numpy as jnp
from jax import lax
from jax.experimental import pallas as pl
from jax.experimental.pallas import tpu as pltpu
from jax.sharding import PartitionSpec as P

SAMPLES = 2048
BAND = 512
FB = 128
TB = 256
BAND_LO = 128
DEC = 8
PAIR = 2
CHUNKS = 2
EARLY = 2

RADIX = 8
SPAN = SAMPLES // RADIX
BINS = BAND // RADIX
TIMES = SAMPLES // 2
FOLD = TIMES // 2
INNER = TIMES // RADIX
HALF_FB = FB // 2

epsilon = 1e-06
full_turn = 2.0 * math.pi
root_half = math.sqrt(0.5)
MESH = pl.DeviceIdType.MESH


COS_HALF = (
    1.4142134965650053, -6.978850988237948, 5.73946117066148, -1.8835629871727047, 0.3106981915530425,
)
SIN_HALF = (
    4.442882834149914, -7.30824115454536, 3.6062889582107696, -0.845763596066154, 0.10920575349257165,
)


def cos_sin(turns):
    x = turns - jnp.round(turns)
    y = x * x
    c, s = COS_HALF[-1], SIN_HALF[-1]
    for c_next, s_next in zip(COS_HALF[-2::-1], SIN_HALF[-2::-1]):
        c = c * y + c_next
        s = s * y + s_next
    return c * c - 1.0, s * x * c


def float_iota(shape, axis):
    return lax.broadcasted_iota(jnp.int32, shape, axis).astype(jnp.float32)


def bit_of(value, at):
    return lax.rem(value // (1 << at), 2)


def flip(value, at):
    return value + (1 - 2 * bit_of(value, at)) * (1 << at)


def split(value):
    high = value.astype(jnp.bfloat16)
    return high, (value - high.astype(jnp.float32)).astype(jnp.bfloat16)


def env_bins(axis):
    shape = (1, FB) if axis else (FB, 1)
    lane = lax.broadcasted_iota(jnp.int32, shape, axis)
    return jnp.where(lane < HALF_FB, 2 * lane + 2, 2 * lane - (FB - 1)).astype(jnp.float32)


def inverse_four(values):
    (ar, ai), (br, bi), (cr, ci), (dr, di) = values
    sr, si, er, ei = ar + cr, ai + ci, ar - cr, ai - ci
    tr, ti, fr, fi = br + dr, bi + di, br - dr, bi - di
    return [(sr + tr, si + ti), (er - fi, ei + fr), (sr - tr, si - ti), (er + fi, ei - fr)]


def kernel(
    n_chan, x_hbm, d_hbm, off_hbm, out_ref,
    d_ref, own, other, fwd, inv, env, fwd_c, fwd_s, inv_c, inv_s, gain, phase_c, phase_s,
    nodes_d, turn_tab, turn_row, e_tab, acc, send_buf, recv_buf,
    off_ref, off_sem, d_sem, x_in, x_send, x_recv, send_sem, recv_sem, round_sem,
):
    chans, nodes = d_ref.shape
    half = own.shape[1]
    kept = own.shape[0] // chans
    group = chans // CHUNKS
    rows = kept * group
    node_rows = nodes // n_chan
    me = lax.axis_index("chan")
    tm = lax.axis_index("tm")
    partner = 1 - tm
    unit = 1.0 / SAMPLES

    rounds = n_chan.bit_length() - 1
    barrier = pltpu.get_barrier_semaphore()
    pl.semaphore_signal(barrier, inc=1, device_id={"tm": partner}, device_id_type=MESH)
    for r in range(rounds):
        pl.semaphore_signal(barrier, inc=1, device_id={"chan": flip(me, r)}, device_id_type=MESH)

    offsets_in = pltpu.make_async_copy(off_hbm, off_ref, off_sem)
    delays_in = pltpu.make_async_copy(d_hbm, d_ref, d_sem)
    delays_in.start()
    offsets_in.start()

    def tell(r):
        if r < rounds:
            pl.semaphore_signal(round_sem.at[r], inc=1, device_id={"chan": flip(me, r)}, device_id_type=MESH)

    def hear(r):
        if r < rounds:
            pl.semaphore_wait(round_sem.at[r], 1)
            tell(r + 1)

    def mine_of(ch):
        return pltpu.make_async_copy(
            x_hbm.at[ch, pl.ds(pl.multiple_of(tm * kept, kept), kept)], own.at[pl.ds(ch * kept, kept)], x_in
        )

    def to_partner(src, dst, at):
        return pltpu.make_async_remote_copy(
            src_ref=src, dst_ref=dst, send_sem=x_send, recv_sem=x_recv.at[at],
            device_id={"tm": partner}, device_id_type=MESH,
        )

    pl.semaphore_wait(barrier, rounds + 1)
    for ch in range(chans):
        to_partner(
            x_hbm.at[ch, pl.ds(pl.multiple_of(partner * kept, kept), kept)],
            other.at[pl.ds(ch * kept, kept)], ch // group,
        ).start()
    tell(0)
    for ch in range(chans):
        mine_of(ch).start()

    late = jnp.where(lax.broadcasted_iota(jnp.int32, (1, SPAN), 1) * 0 + tm == 1, -1.0, 1.0)
    residue = lax.broadcasted_iota(jnp.int32, (RADIX, SPAN), 0)
    c, s = cos_sin(residue.astype(jnp.float32) * float_iota((RADIX, SPAN), 1) * unit)
    sign = jnp.where((residue & 1) == 1, late, 1.0)
    fwd_c[...] = c * sign
    fwd_s[...] = s * sign
    inv_c[...], inv_s[...] = cos_sin(float_iota((RADIX, INNER), 0) * float_iota((RADIX, INNER), 1) * (1.0 / TIMES))
    lane = lax.broadcasted_iota(jnp.int32, (1, 2 * BINS), 1)
    quarter = jnp.where(lane < BINS, 0.0, 0.25)
    place = jnp.where(lane < BINS, lane, lane - BINS).astype(jnp.float32)
    _, s = cos_sin((RADIX * place + float_iota((RADIX, 2 * BINS), 0) + 0.5) * (0.5 / BAND))
    gain[...] = s * s * (2.0 / SAMPLES)

    def forward_table(at):
        first = pl.multiple_of(at * 32, 32)
        spot = float_iota((32, 2 * BINS), 0) + first.astype(jnp.float32)
        c, s = cos_sin(spot * ((place + BAND_LO // RADIX) * (1.0 / SPAN)) + quarter)
        for value, base in ((c, 0), (s, SPAN)):
            high, low = split(value)
            fwd[0, pl.ds(pl.multiple_of(base + first, 32), 32), :] = high
            fwd[1, pl.ds(pl.multiple_of(base + first, 32), 32), :] = low

    pl.loop(0, SPAN // 32)(forward_table)

    row = lax.broadcasted_iota(jnp.int32, (2 * BINS, 1), 0)
    row_quarter = jnp.where(row < BINS, 0.0, 0.25)
    row_place = jnp.where(row < BINS, row, row - BINS).astype(jnp.float32)
    c, s = cos_sin(row_place * (float_iota((1, INNER), 1) * (1.0 / INNER)) + row_quarter)
    for base in (0, 2 * BINS):
        inv[0, base : base + 2 * BINS, :] = c.astype(jnp.bfloat16)
        inv[1, base : base + 2 * BINS, :] = s.astype(jnp.bfloat16)

    env_lane = lax.broadcasted_iota(jnp.int32, (1, FB), 1)
    env_quarter = jnp.where(env_lane < HALF_FB, 0.0, 0.25)
    env_place = jnp.where(env_lane < HALF_FB, env_lane, env_lane - HALF_FB).astype(jnp.float32)
    for odd in range(2):
        freq = (2.0 * env_place + (1.0 if odd else 2.0)) * (1.0 / TIMES)
        base_c, base_s = cos_sin(float_iota((32, FB), 0) * freq + env_quarter)
        lead_c, lead_s = cos_sin(float_iota((FOLD // 32, FB), 0) * (freq * 32.0))
        for a in range(FOLD // 32):
            value = lead_c[a : a + 1] * base_c - lead_s[a : a + 1] * base_s
            env[odd, a * 32 : (a + 1) * 32, :] = value.astype(jnp.bfloat16)

    hear(0)

    delays_in.wait()
    nodes_d[...] = (d_ref[...].astype(jnp.float32) * unit).T
    block = PAIR * node_rows
    bins = env_bins(1)
    pairs = n_chan // PAIR

    def phases(step):
        at = pl.ds(pl.multiple_of(step * block, block), block)
        delay = nodes_d[at, :]
        for ch in range(chans):
            c, s = cos_sin(delay[:, ch : ch + 1] * bins)
            phase_c[ch, at, :] = c
            phase_s[ch, at, :] = s

    def two_phases(step):
        phases(2 * step)
        phases(2 * step + 1)

    pl.loop(0, pairs // 4)(two_phases)
    hear(1)
    pl.loop(pairs // 4, pairs // 2)(two_phases)
    hear(2)

    turns = env_bins(0)
    c, s = cos_sin(turns * (float_iota((1, TB), 1) * (DEC * unit)))
    for first, value in ((0, c), (FB, -s)):
        for piece, part in enumerate(split(value)):
            turn_tab[first : first + FB, piece * TB : (piece + 1) * TB] = part
    offsets_in.wait()
    for w in range(kept):
        shift = off_ref[w].astype(jnp.float32) * unit
        turn_row[w, :, :FB], turn_row[w, :, FB:] = cos_sin(bins * shift)

    pltpu.make_async_copy(own, own, x_in).wait()

    def envelope(g):
        at = pl.ds(pl.multiple_of(g * rows, rows), rows)
        mine = own[at, :].astype(jnp.float32)
        theirs = other[at, :].astype(jnp.float32)
        a, b = [], []
        for q in range(RADIX // 2):
            cols = slice(q * SPAN, (q + 1) * SPAN)
            a.append(mine[:, cols] + theirs[:, cols])
            b.append(mine[:, cols] - theirs[:, cols])
        s02, d02, s13, d13 = a[0] + a[2], a[0] - a[2], a[1] + a[3], a[1] - a[3]
        t, u = (b[1] - b[3]) * root_half, (b[1] + b[3]) * root_half
        one = (b[0] + t, -(u + b[2]))
        three = (b[0] - t, b[2] - u)
        parts = [
            (s02 + s13, None), one, (d02, -d13), three,
            (s02 - s13, None), (three[0], -three[1]), (d02, d13), (one[0], -one[1]),
        ]
        stacked = []
        for r, (re, im) in enumerate(parts):
            if r == 0:
                zr, zi = re, jnp.zeros_like(re)
            else:
                c, s = fwd_c[r : r + 1, :], fwd_s[r : r + 1, :]
                if im is None:
                    zr, zi = re * c, -(re * s)
                else:
                    zr, zi = re * c + im * s, im * c - re * s
            stacked.append(jnp.concatenate([zr, zi], axis=1).astype(jnp.bfloat16))
        spectrum = jnp.dot(
            jnp.concatenate(stacked, axis=0), jnp.concatenate([fwd[0], fwd[1]], axis=1), preferred_element_type=jnp.float32
        )
        spectrum = spectrum[:, : 2 * BINS] + spectrum[:, 2 * BINS :]
        tapered = []
        for r in range(RADIX):
            high, low = split(spectrum[r * rows : (r + 1) * rows] * gain[r : r + 1, :])
            tapered.append(jnp.concatenate([high, low], axis=1))
        inner = jnp.dot(jnp.concatenate(tapered, axis=0), jnp.concatenate([inv[0], inv[1]], axis=1), preferred_element_type=jnp.float32)
        turned = []
        for r in range(RADIX):
            re = inner[r * rows : (r + 1) * rows, :INNER]
            im = inner[r * rows : (r + 1) * rows, INNER:]
            if r:
                c, s = inv_c[r : r + 1, :], inv_s[r : r + 1, :]
                re, im = re * c - im * s, re * s + im * c
            turned.append((re, im))
        evens, odds = inverse_four(turned[0::2]), inverse_four(turned[1::2])
        same, cross = [], []
        for q in range(RADIX // 2):
            (er, ei), (fr, fi) = evens[q], odds[q]
            same.append((er * er + ei * ei) + (fr * fr + fi * fi))
            if q == 0:
                both = 2.0 * (er * fr + ei * fi)
            elif q == 1:
                both = (2.0 * root_half) * (er * (fr - fi) + ei * (fr + fi))
            elif q == 2:
                both = 2.0 * (ei * fr - er * fi)
            else:
                both = (2.0 * root_half) * (ei * (fr - fi) - er * (fr + fi))
            cross.append(both)
        total = jnp.sum((same[0] + same[1]) + (same[2] + same[3]), axis=1, keepdims=True)
        even = jnp.dot(
            jnp.concatenate(same, axis=1).astype(jnp.bfloat16), env[0], preferred_element_type=jnp.float32
        )
        odd = jnp.dot(
            jnp.concatenate(cross, axis=1).astype(jnp.bfloat16), env[1], preferred_element_type=jnp.float32
        )
        factor = 4.0 / (math.sqrt(SAMPLES) * (total * (4.0 / SAMPLES) + epsilon))
        even, odd = even * factor, odd * factor
        lower = lax.broadcasted_iota(jnp.int32, (1, FB), 1) < HALF_FB
        e_tab[g, :, :FB] = jnp.where(lower, even, pltpu.roll(odd, HALF_FB, 1))
        e_tab[g, :, FB:] = jnp.where(lower, pltpu.roll(even, HALF_FB, 1), odd)

    def outgoing(dest):
        return pltpu.make_async_remote_copy(
            src_ref=send_buf.at[dest],
            dst_ref=recv_buf.at[me],
            send_sem=send_sem,
            recv_sem=recv_sem.at[me],
            device_id={"chan": dest},
            device_id_type=MESH,
        )

    def send_pair(pair):
        for side in range(PAIR):
            dest = pair * PAIR + side

            @pl.when(dest != me)
            def _():
                outgoing(dest).start()

    def stack_up(g, pair, sums):
        at = pl.ds(pl.multiple_of(pair * block, block), block)
        for ch in range(group):
            pc = phase_c[g * group + ch, at, :]
            ps = phase_s[g * group + ch, at, :]
            for w in range(kept):
                r = kept * ch + w
                er, ei = e_tab[g, r : r + 1, :FB], e_tab[g, r : r + 1, FB:]
                sums[0][w] = sums[0][w] + (pc * er - ps * ei)
                sums[1][w] = sums[1][w] + (pc * ei + ps * er)
        return sums

    def pack(pair, sums):
        for side in range(PAIR):
            part = slice(side * node_rows, (side + 1) * node_rows)
            packed = jnp.concatenate([sums[p][w][part] for p in range(2) for w in range(kept)], axis=0)
            send_buf[pair * PAIR + side] = packed.astype(jnp.bfloat16)

    acc[...] = jnp.zeros_like(acc)

    @pl.loop(0, CHUNKS)
    def _(g):
        arrived = other.at[pl.ds(pl.multiple_of(g * rows, rows), rows)]
        to_partner(arrived, arrived, g).wait_recv()
        envelope(g)
        for step in range(EARLY):
            sums = stack_up(g, step, [[acc[step, p * kept + w] for w in range(kept)] for p in range(2)])
            for p in range(2):
                for w in range(kept):
                    acc[step, p * kept + w] = sums[p][w]

            @pl.when(g == CHUNKS - 1)
            def _():
                pack(step, sums)
                if step:
                    for r in range(3, rounds):
                        hear(r)
                    send_pair(step - 1)

    @pl.loop(EARLY, pairs)
    def _(step):
        sums = [[jnp.zeros((block, FB), jnp.float32) for _ in range(kept)] for _ in range(2)]
        for g in range(CHUNKS):
            sums = stack_up(g, step, sums)
        pack(step, sums)
        send_pair(step - 1)

    send_pair(pairs - 1)

    def incoming(source):
        return pltpu.make_async_remote_copy(
            src_ref=send_buf.at[source],
            dst_ref=recv_buf.at[source],
            send_sem=send_sem,
            recv_sem=recv_sem.at[source],
            device_id={"chan": source},
            device_id_type=MESH,
        )

    def add_one(step, stack):
        source = lax.rem(me + step, n_chan)
        incoming(source).wait_recv()
        return stack + recv_buf[source].astype(jnp.float32)

    stack = lax.fori_loop(1, n_chan, add_one, send_buf[me].astype(jnp.float32))

    turned = []
    for w in range(kept):
        c, s = turn_row[w, :, :FB], turn_row[w, :, FB:]
        re = stack[w * node_rows : (w + 1) * node_rows]
        im = stack[(kept + w) * node_rows : (kept + w + 1) * node_rows]
        turned.append(jnp.concatenate([re * c - im * s, re * s + im * c], axis=1))
    high, low = split(jnp.concatenate(turned, axis=0))
    bright = jnp.dot(
        jnp.concatenate([high, low], axis=0), turn_tab[...], preferred_element_type=jnp.float32
    )
    size = kept * node_rows
    bright = bright[:size, :TB] + (bright[:size, TB:] + bright[size:, :TB])
    scale = 1.0 / math.sqrt(FB * chans * n_chan)
    out_ref[...] = (bright * scale).reshape(kept, node_rows, TB)

    to_partner(other, other, 0).wait_send()
    pltpu.make_async_remote_copy(
        src_ref=send_buf.at[pl.ds(0, n_chan - 1)],
        dst_ref=recv_buf.at[pl.ds(0, n_chan - 1)],
        send_sem=send_sem,
        recv_sem=recv_sem.at[0],
        device_id={"chan": flip(me, 0)},
        device_id_type=MESH,
    ).wait_send()


def solution(mesh):
    n_chan = mesh.shape["chan"]

    def on_device(traces, delays, offsets):
        chans, windows, half = traces.shape
        nodes = delays.shape[0]
        kept = offsets.shape[0]
        node_rows = nodes // n_chan
        block = PAIR * node_rows
        packed_rows = 2 * kept * node_rows
        hbm = pl.BlockSpec(memory_space=pltpu.HBM)
        return pl.pallas_call(
            functools.partial(kernel, n_chan),
            out_shape=jax.ShapeDtypeStruct((kept, node_rows, TB), jnp.float32),
            in_specs=[hbm] * 3,
            out_specs=pl.BlockSpec(memory_space=pltpu.VMEM),
            scratch_shapes=[
                pltpu.VMEM((chans, nodes), jnp.int32),
                pltpu.VMEM((chans * kept, half), jnp.bfloat16),
                pltpu.VMEM((chans * kept, half), jnp.bfloat16),
                pltpu.VMEM((2, 2 * SPAN, 2 * BINS), jnp.bfloat16),
                pltpu.VMEM((2, 4 * BINS, INNER), jnp.bfloat16),
                pltpu.VMEM((2, FOLD, FB), jnp.bfloat16),
                pltpu.VMEM((RADIX, SPAN), jnp.float32),
                pltpu.VMEM((RADIX, SPAN), jnp.float32),
                pltpu.VMEM((RADIX, INNER), jnp.float32),
                pltpu.VMEM((RADIX, INNER), jnp.float32),
                pltpu.VMEM((RADIX, 2 * BINS), jnp.float32),
                pltpu.VMEM((chans, nodes, FB), jnp.float32),
                pltpu.VMEM((chans, nodes, FB), jnp.float32),
                pltpu.VMEM((nodes, chans), jnp.float32),
                pltpu.VMEM((2 * FB, 2 * TB), jnp.bfloat16),
                pltpu.VMEM((kept, 1, 2 * FB), jnp.float32),
                pltpu.VMEM((CHUNKS, kept * chans // CHUNKS, 2 * FB), jnp.float32),
                pltpu.VMEM((EARLY, 2 * kept, block, FB), jnp.float32),
                pltpu.VMEM((n_chan, packed_rows, FB), jnp.bfloat16),
                pltpu.VMEM((n_chan, packed_rows, FB), jnp.bfloat16),
                pltpu.SMEM((kept,), jnp.int32),
                pltpu.SemaphoreType.DMA,
                pltpu.SemaphoreType.DMA,
                pltpu.SemaphoreType.DMA,
                pltpu.SemaphoreType.DMA,
                pltpu.SemaphoreType.DMA((CHUNKS,)),
                pltpu.SemaphoreType.DMA,
                pltpu.SemaphoreType.DMA((n_chan,)),
                pltpu.SemaphoreType.REGULAR((n_chan.bit_length() - 1,)),
            ],
            compiler_params=pltpu.CompilerParams(
                collective_id=0, has_side_effects=True, vmem_limit_bytes=16 * 1024 * 1024 + 8 * chans * nodes * FB
            ),
        )(*(pltpu.with_memory_space_constraint(a, pltpu.HBM) for a in (traces, delays.T, offsets)))

    placed = (P("chan", None, "tm"), P(None, "chan"), P("tm"))
    return jax.shard_map(
        on_device, mesh=mesh, in_specs=placed, out_specs=P("tm", "chan", None), check_vma=False
    )
```

```python
import functools
import math

import jax
import jax.numpy as jnp
from jax import lax
from jax.experimental import pallas as pl
from jax.experimental.pallas import tpu as pltpu
from jax.sharding import PartitionSpec as P

SAMPLES = 2048
BAND = 512
FB = 128
TB = 256
BAND_LO = 128
DEC = 8
UNROLL = 4
CHUNKS = 2
EARLY = 2

RADIX = 8
SPAN = SAMPLES // RADIX
BINS = BAND // RADIX
TIMES = SAMPLES // 2
FOLD = TIMES // 2
INNER = TIMES // RADIX
HALF_FB = FB // 2

epsilon = 1e-06
full_turn = 2.0 * math.pi
root_half = math.sqrt(0.5)
MESH = pl.DeviceIdType.MESH


COS_HALF = (
    1.4142134965650053, -6.978850988237948, 5.73946117066148, -1.8835629871727047, 0.3106981915530425,
)
SIN_HALF = (
    4.442882834149914, -7.30824115454536, 3.6062889582107696, -0.845763596066154, 0.10920575349257165,
)


def cos_sin(turns):
    x = turns - jnp.round(turns)
    y = x * x
    c, s = COS_HALF[-1], SIN_HALF[-1]
    for c_next, s_next in zip(COS_HALF[-2::-1], SIN_HALF[-2::-1]):
        c = c * y + c_next
        s = s * y + s_next
    return c * c - 1.0, s * x * c


def float_iota(shape, axis):
    return lax.broadcasted_iota(jnp.int32, shape, axis).astype(jnp.float32)


def bit_of(value, at):
    return lax.rem(value // (1 << at), 2)


def flip(value, at):
    return value + (1 - 2 * bit_of(value, at)) * (1 << at)


def split(value):
    high = value.astype(jnp.bfloat16)
    return high, (value - high.astype(jnp.float32)).astype(jnp.bfloat16)


def env_bins(axis):
    shape = (1, FB) if axis else (FB, 1)
    lane = lax.broadcasted_iota(jnp.int32, shape, axis)
    return jnp.where(lane < HALF_FB, 2 * lane + 2, 2 * lane - (FB - 1)).astype(jnp.float32)


def inverse_four(values):
    (ar, ai), (br, bi), (cr, ci), (dr, di) = values
    sr, si, er, ei = ar + cr, ai + ci, ar - cr, ai - ci
    tr, ti, fr, fi = br + dr, bi + di, br - dr, bi - di
    return [(sr + tr, si + ti), (er - fi, ei + fr), (sr - tr, si - ti), (er + fi, ei - fr)]


def kernel(
    n_chan, x_hbm, d_hbm, off_hbm, out_ref,
    d_ref, own, other, fwd, inv, env, fwd_c, fwd_s, inv_c, inv_s, gain, phase_c, phase_s,
    nodes_d, turn_tab, turn_row, e_tab, acc, send_buf, recv_buf,
    off_ref, off_sem, d_sem, x_in, x_send, x_recv, send_sem, recv_sem, round_sem,
):
    chans, nodes = d_ref.shape
    half = own.shape[1]
    kept = own.shape[0] // chans
    group = chans // CHUNKS
    rows = kept * group
    node_rows = nodes // n_chan
    me = lax.axis_index("chan")
    tm = lax.axis_index("tm")
    partner = 1 - tm
    unit = 1.0 / SAMPLES

    rounds = n_chan.bit_length() - 1
    barrier = pltpu.get_barrier_semaphore()
    pl.semaphore_signal(barrier, inc=1, device_id={"tm": partner}, device_id_type=MESH)
    for r in range(rounds):
        pl.semaphore_signal(barrier, inc=1, device_id={"chan": flip(me, r)}, device_id_type=MESH)

    offsets_in = pltpu.make_async_copy(off_hbm, off_ref, off_sem)
    delays_in = pltpu.make_async_copy(d_hbm, d_ref, d_sem)
    delays_in.start()
    offsets_in.start()

    def tell(r):
        if r < rounds:
            pl.semaphore_signal(round_sem.at[r], inc=1, device_id={"chan": flip(me, r)}, device_id_type=MESH)

    def hear(r):
        if r < rounds:
            pl.semaphore_wait(round_sem.at[r], 1)
            tell(r + 1)

    def mine_of(ch):
        return pltpu.make_async_copy(
            x_hbm.at[ch, pl.ds(pl.multiple_of(tm * kept, kept), kept)], own.at[pl.ds(ch * kept, kept)], x_in
        )

    def to_partner(src, dst, at):
        return pltpu.make_async_remote_copy(
            src_ref=src, dst_ref=dst, send_sem=x_send, recv_sem=x_recv.at[at],
            device_id={"tm": partner}, device_id_type=MESH,
        )

    pl.semaphore_wait(barrier, rounds + 1)
    for ch in range(chans):
        to_partner(
            x_hbm.at[ch, pl.ds(pl.multiple_of(partner * kept, kept), kept)],
            other.at[pl.ds(ch * kept, kept)], ch // group,
        ).start()
    tell(0)
    for ch in range(chans):
        mine_of(ch).start()

    late = jnp.where(lax.broadcasted_iota(jnp.int32, (1, SPAN), 1) * 0 + tm == 1, -1.0, 1.0)
    residue = lax.broadcasted_iota(jnp.int32, (RADIX, SPAN), 0)
    c, s = cos_sin(residue.astype(jnp.float32) * float_iota((RADIX, SPAN), 1) * unit)
    sign = jnp.where((residue & 1) == 1, late, 1.0)
    fwd_c[...] = c * sign
    fwd_s[...] = s * sign
    inv_c[...], inv_s[...] = cos_sin(float_iota((RADIX, INNER), 0) * float_iota((RADIX, INNER), 1) * (1.0 / TIMES))
    lane = lax.broadcasted_iota(jnp.int32, (1, 2 * BINS), 1)
    quarter = jnp.where(lane < BINS, 0.0, 0.25)
    place = jnp.where(lane < BINS, lane, lane - BINS).astype(jnp.float32)
    _, s = cos_sin((RADIX * place + float_iota((RADIX, 2 * BINS), 0) + 0.5) * (0.5 / BAND))
    gain[...] = s * s * (2.0 / SAMPLES)

    def forward_table(at):
        first = pl.multiple_of(at * 32, 32)
        spot = float_iota((32, 2 * BINS), 0) + first.astype(jnp.float32)
        c, s = cos_sin(spot * ((place + BAND_LO // RADIX) * (1.0 / SPAN)) + quarter)
        for value, base in ((c, 0), (s, SPAN)):
            fwd[pl.ds(pl.multiple_of(base + first, 32), 32), :] = value.astype(jnp.bfloat16)

    pl.loop(0, SPAN // 32)(forward_table)

    row = lax.broadcasted_iota(jnp.int32, (2 * BINS, 1), 0)
    row_quarter = jnp.where(row < BINS, 0.0, 0.25)
    row_place = jnp.where(row < BINS, row, row - BINS).astype(jnp.float32)
    c, s = cos_sin(row_place * (float_iota((1, INNER), 1) * (1.0 / INNER)) + row_quarter)
    for base in (0, 2 * BINS):
        inv[0, base : base + 2 * BINS, :] = c.astype(jnp.bfloat16)
        inv[1, base : base + 2 * BINS, :] = s.astype(jnp.bfloat16)

    env_lane = lax.broadcasted_iota(jnp.int32, (1, FB), 1)
    env_place = jnp.where(env_lane < HALF_FB, env_lane, env_lane - HALF_FB).astype(jnp.float32)
    for odd in range(2):
        freq = (2.0 * env_place + (1.0 if odd else 2.0)) * (1.0 / TIMES)
        base_c, base_s = cos_sin(float_iota((32, FB), 0) * freq)
        lead_c, lead_s = cos_sin(float_iota((FOLD // 32, FB), 0) * (freq * 32.0))
        shown = (env_lane >= HALF_FB) == bool(odd)
        base_c, base_s = jnp.where(shown, base_c, 0.0), jnp.where(shown, base_s, 0.0)
        for a in range(FOLD // 32):
            lc, ls = lead_c[a : a + 1], lead_s[a : a + 1]
            at = slice(odd * FOLD + a * 32, odd * FOLD + (a + 1) * 32)
            env[0, at, :] = (lc * base_c - ls * base_s).astype(jnp.bfloat16)
            env[1, at, :] = -(ls * base_c + lc * base_s).astype(jnp.bfloat16)

    hear(0)

    delays_in.wait()
    nodes_d[...] = (d_ref[...].astype(jnp.float32) * unit).T
    bins = env_bins(1)

    def phases(step):
        at = pl.ds(pl.multiple_of(step * node_rows, node_rows), node_rows)
        delay = nodes_d[at, :]
        for ch in range(chans):
            c, s = cos_sin(delay[:, ch : ch + 1] * bins)
            phase_c[ch, at, :] = c
            phase_s[ch, at, :] = s

    def more_phases(step):
        for k in range(UNROLL):
            phases(UNROLL * step + k)

    steps = n_chan // UNROLL
    pl.loop(0, steps // 2)(more_phases)
    hear(1)
    pl.loop(steps // 2, steps)(more_phases)
    hear(2)

    turns = env_bins(0)
    c, s = cos_sin(turns * (float_iota((1, TB), 1) * (DEC * unit)))
    for first, value in ((0, c), (FB, -s)):
        for piece, part in enumerate(split(value)):
            turn_tab[first : first + FB, piece * TB : (piece + 1) * TB] = part
    offsets_in.wait()
    for w in range(kept):
        shift = off_ref[w].astype(jnp.float32) * unit
        turn_row[w, :, :FB], turn_row[w, :, FB:] = cos_sin(bins * shift)

    pltpu.make_async_copy(own, own, x_in).wait()

    def envelope(g):
        at = pl.ds(pl.multiple_of(g * rows, rows), rows)
        mine = own[at, :].astype(jnp.float32)
        theirs = other[at, :].astype(jnp.float32)
        a, b = [], []
        for q in range(RADIX // 2):
            cols = slice(q * SPAN, (q + 1) * SPAN)
            a.append(mine[:, cols] + theirs[:, cols])
            b.append(mine[:, cols] - theirs[:, cols])
        s02, d02, s13, d13 = a[0] + a[2], a[0] - a[2], a[1] + a[3], a[1] - a[3]
        t, u = (b[1] - b[3]) * root_half, (b[1] + b[3]) * root_half
        one = (b[0] + t, -(u + b[2]))
        three = (b[0] - t, b[2] - u)
        parts = [
            (s02 + s13, None), one, (d02, -d13), three,
            (s02 - s13, None), (three[0], -three[1]), (d02, d13), (one[0], -one[1]),
        ]
        stacked = []
        for r, (re, im) in enumerate(parts):
            if r == 0:
                zr, zi = re, jnp.zeros_like(re)
            else:
                c, s = fwd_c[r : r + 1, :], fwd_s[r : r + 1, :]
                if im is None:
                    zr, zi = re * c, -(re * s)
                else:
                    zr, zi = re * c + im * s, im * c - re * s
            stacked.append(jnp.concatenate([zr, zi], axis=1).astype(jnp.bfloat16))
        spectrum = jnp.dot(
            jnp.concatenate(stacked, axis=0), fwd[...], preferred_element_type=jnp.float32
        )
        tapered = []
        for r in range(RADIX):
            high, low = split(spectrum[r * rows : (r + 1) * rows] * gain[r : r + 1, :])
            tapered.append(jnp.concatenate([high, low], axis=1))
        inner = jnp.dot(jnp.concatenate(tapered, axis=0), jnp.concatenate([inv[0], inv[1]], axis=1), preferred_element_type=jnp.float32)
        turned = []
        for r in range(RADIX):
            re = inner[r * rows : (r + 1) * rows, :INNER]
            im = inner[r * rows : (r + 1) * rows, INNER:]
            if r:
                c, s = inv_c[r : r + 1, :], inv_s[r : r + 1, :]
                re, im = re * c - im * s, re * s + im * c
            turned.append((re, im))
        evens, odds = inverse_four(turned[0::2]), inverse_four(turned[1::2])
        same, cross = [], []
        for q in range(RADIX // 2):
            (er, ei), (fr, fi) = evens[q], odds[q]
            same.append((er * er + ei * ei) + (fr * fr + fi * fi))
            if q == 0:
                both = 2.0 * (er * fr + ei * fi)
            elif q == 1:
                both = (2.0 * root_half) * (er * (fr - fi) + ei * (fr + fi))
            elif q == 2:
                both = 2.0 * (ei * fr - er * fi)
            else:
                both = (2.0 * root_half) * (ei * (fr - fi) - er * (fr + fi))
            cross.append(both)
        total = jnp.sum((same[0] + same[1]) + (same[2] + same[3]), axis=1, keepdims=True)
        spread = jnp.dot(
            jnp.concatenate(same + cross, axis=1).astype(jnp.bfloat16),
            jnp.concatenate([env[0], env[1]], axis=1), preferred_element_type=jnp.float32,
        )
        factor = 4.0 / (math.sqrt(SAMPLES) * (total * (4.0 / SAMPLES) + epsilon))
        e_tab[g] = spread * factor

    def outgoing(dest):
        return pltpu.make_async_remote_copy(
            src_ref=send_buf.at[dest],
            dst_ref=recv_buf.at[me],
            send_sem=send_sem,
            recv_sem=recv_sem.at[me],
            device_id={"chan": dest},
            device_id_type=MESH,
        )

    def send(dest):
        @pl.when(dest != me)
        def _():
            outgoing(dest).start()

    def stack_up(g, dest, sums):
        at = pl.ds(pl.multiple_of(dest * node_rows, node_rows), node_rows)
        for ch in range(group):
            pc = phase_c[g * group + ch, at, :]
            ps = phase_s[g * group + ch, at, :]
            for w in range(kept):
                r = kept * ch + w
                er, ei = e_tab[g, r : r + 1, :FB], e_tab[g, r : r + 1, FB:]
                sums[0][w] = sums[0][w] + (pc * er - ps * ei)
                sums[1][w] = sums[1][w] + (pc * ei + ps * er)
        return sums

    def pack(dest, sums):
        packed = jnp.concatenate([sums[p][w] for p in range(2) for w in range(kept)], axis=0)
        send_buf[dest] = packed.astype(jnp.bfloat16)

    acc[...] = jnp.zeros_like(acc)

    @pl.loop(0, CHUNKS)
    def _(g):
        arrived = other.at[pl.ds(pl.multiple_of(g * rows, rows), rows)]
        to_partner(arrived, arrived, g).wait_recv()
        envelope(g)
        for step in range(EARLY):
            sums = stack_up(g, step, [[acc[step, p * kept + w] for w in range(kept)] for p in range(2)])
            for p in range(2):
                for w in range(kept):
                    acc[step, p * kept + w] = sums[p][w]

            @pl.when(g == CHUNKS - 1)
            def _():
                pack(step, sums)
                if step == 1:
                    for r in range(3, rounds):
                        hear(r)
                if step:
                    send(step - 1)

    @pl.loop(EARLY, n_chan)
    def _(step):
        sums = [[jnp.zeros((node_rows, FB), jnp.float32) for _ in range(kept)] for _ in range(2)]
        for g in range(CHUNKS):
            sums = stack_up(g, step, sums)
        pack(step, sums)
        send(step - 1)

    send(n_chan - 1)

    def incoming(source):
        return pltpu.make_async_remote_copy(
            src_ref=send_buf.at[source],
            dst_ref=recv_buf.at[source],
            send_sem=send_sem,
            recv_sem=recv_sem.at[source],
            device_id={"chan": source},
            device_id_type=MESH,
        )

    def add_one(step, stack):
        source = lax.rem(me + step, n_chan)
        incoming(source).wait_recv()
        return stack + recv_buf[source].astype(jnp.float32)

    stack = lax.fori_loop(1, n_chan, add_one, send_buf[me].astype(jnp.float32))

    turned = []
    for w in range(kept):
        c, s = turn_row[w, :, :FB], turn_row[w, :, FB:]
        re = stack[w * node_rows : (w + 1) * node_rows]
        im = stack[(kept + w) * node_rows : (kept + w + 1) * node_rows]
        turned.append(jnp.concatenate([re * c - im * s, re * s + im * c], axis=1))
    high, low = split(jnp.concatenate(turned, axis=0))
    bright = jnp.dot(
        jnp.concatenate([high, low], axis=0), turn_tab[...], preferred_element_type=jnp.float32
    )
    size = kept * node_rows
    bright = bright[:size, :TB] + (bright[:size, TB:] + bright[size:, :TB])
    scale = 1.0 / math.sqrt(FB * chans * n_chan)
    out_ref[...] = (bright * scale).reshape(kept, node_rows, TB)

    to_partner(other, other, 0).wait_send()
    pltpu.make_async_remote_copy(
        src_ref=send_buf.at[pl.ds(0, n_chan - 1)],
        dst_ref=recv_buf.at[pl.ds(0, n_chan - 1)],
        send_sem=send_sem,
        recv_sem=recv_sem.at[0],
        device_id={"chan": flip(me, 0)},
        device_id_type=MESH,
    ).wait_send()


def solution(mesh):
    n_chan = mesh.shape["chan"]

    def on_device(traces, delays, offsets):
        chans, windows, half = traces.shape
        nodes = delays.shape[0]
        kept = offsets.shape[0]
        node_rows = nodes // n_chan
        packed_rows = 2 * kept * node_rows
        hbm = pl.BlockSpec(memory_space=pltpu.HBM)
        return pl.pallas_call(
            functools.partial(kernel, n_chan),
            out_shape=jax.ShapeDtypeStruct((kept, node_rows, TB), jnp.float32),
            in_specs=[hbm] * 3,
            out_specs=pl.BlockSpec(memory_space=pltpu.VMEM),
            scratch_shapes=[
                pltpu.VMEM((chans, nodes), jnp.int32),
                pltpu.VMEM((chans * kept, half), jnp.bfloat16),
                pltpu.VMEM((chans * kept, half), jnp.bfloat16),
                pltpu.VMEM((2 * SPAN, 2 * BINS), jnp.bfloat16),
                pltpu.VMEM((2, 4 * BINS, INNER), jnp.bfloat16),
                pltpu.VMEM((2, TIMES, FB), jnp.bfloat16),
                pltpu.VMEM((RADIX, SPAN), jnp.float32),
                pltpu.VMEM((RADIX, SPAN), jnp.float32),
                pltpu.VMEM((RADIX, INNER), jnp.float32),
                pltpu.VMEM((RADIX, INNER), jnp.float32),
                pltpu.VMEM((RADIX, 2 * BINS), jnp.float32),
                pltpu.VMEM((chans, nodes, FB), jnp.float32),
                pltpu.VMEM((chans, nodes, FB), jnp.float32),
                pltpu.VMEM((nodes, chans), jnp.float32),
                pltpu.VMEM((2 * FB, 2 * TB), jnp.bfloat16),
                pltpu.VMEM((kept, 1, 2 * FB), jnp.float32),
                pltpu.VMEM((CHUNKS, kept * chans // CHUNKS, 2 * FB), jnp.float32),
                pltpu.VMEM((EARLY, 2 * kept, node_rows, FB), jnp.float32),
                pltpu.VMEM((n_chan, packed_rows, FB), jnp.bfloat16),
                pltpu.VMEM((n_chan, packed_rows, FB), jnp.bfloat16),
                pltpu.SMEM((kept,), jnp.int32),
                pltpu.SemaphoreType.DMA,
                pltpu.SemaphoreType.DMA,
                pltpu.SemaphoreType.DMA,
                pltpu.SemaphoreType.DMA,
                pltpu.SemaphoreType.DMA((CHUNKS,)),
                pltpu.SemaphoreType.DMA,
                pltpu.SemaphoreType.DMA((n_chan,)),
                pltpu.SemaphoreType.REGULAR((n_chan.bit_length() - 1,)),
            ],
            compiler_params=pltpu.CompilerParams(
                collective_id=0, has_side_effects=True, vmem_limit_bytes=16 * 1024 * 1024 + 8 * chans * nodes * FB
            ),
        )(*(pltpu.with_memory_space_constraint(a, pltpu.HBM) for a in (traces, delays.T, offsets)))

    placed = (P("chan", None, "tm"), P(None, "chan"), P("tm"))
    return jax.shard_map(
        on_device, mesh=mesh, in_specs=placed, out_specs=P("tm", "chan", None), check_vma=False
    )
```

```python
import functools
import math

import jax
import jax.numpy as jnp
from jax import lax
from jax.experimental import pallas as pl
from jax.experimental.pallas import tpu as pltpu
from jax.sharding import PartitionSpec as P

SAMPLES = 2048
BAND = 512
FB = 128
TB = 256
BAND_LO = 128
DEC = 8
UNROLL = 4
CHUNKS = 2
EARLY = 2

RADIX = 8
ORDER = (0, 4, 2, 6, 1, 5, 3, 7)
TILE = 16
SPAN = SAMPLES // RADIX
BINS = BAND // RADIX
TIMES = SAMPLES // 2
FOLD = TIMES // 2
INNER = TIMES // RADIX
HALF_FB = FB // 2

epsilon = 1e-06
full_turn = 2.0 * math.pi
root_half = math.sqrt(0.5)
MESH = pl.DeviceIdType.MESH


COS_HALF = (
    1.4142134965650053, -6.978850988237948, 5.73946117066148, -1.8835629871727047, 0.3106981915530425,
)
SIN_HALF = (
    4.442882834149914, -7.30824115454536, 3.6062889582107696, -0.845763596066154, 0.10920575349257165,
)


def cos_sin(turns):
    x = turns - jnp.round(turns)
    y = x * x
    c, s = COS_HALF[-1], SIN_HALF[-1]
    for c_next, s_next in zip(COS_HALF[-2::-1], SIN_HALF[-2::-1]):
        c = c * y + c_next
        s = s * y + s_next
    return c * c - 1.0, s * x * c


def float_iota(shape, axis):
    return lax.broadcasted_iota(jnp.int32, shape, axis).astype(jnp.float32)


def bit_of(value, at):
    return lax.rem(value // (1 << at), 2)


def flip(value, at):
    return value ^ (1 << at)


def split(value):
    high = value.astype(jnp.bfloat16)
    return high, (value - high.astype(jnp.float32)).astype(jnp.bfloat16)


def env_bins(axis):
    shape = (1, FB) if axis else (FB, 1)
    lane = lax.broadcasted_iota(jnp.int32, shape, axis)
    return jnp.where(lane < HALF_FB, 2 * lane + 2, 2 * lane - (FB - 1)).astype(jnp.float32)


def inverse_four(values):
    (ar, ai), (br, bi), (cr, ci), (dr, di) = values
    sr, si, er, ei = ar + cr, ai + ci, ar - cr, ai - ci
    tr, ti, fr, fi = br + dr, bi + di, br - dr, bi - di
    return [(sr + tr, si + ti), (er - fi, ei + fr), (sr - tr, si - ti), (er + fi, ei - fr)]


def kernel(
    n_chan, x_hbm, d_hbm, off_hbm, out_ref,
    d_ref, own, other, fwd, inv, env, fwd_c, fwd_s, inv_c, inv_s, gain, phase_c, phase_s,
    nodes_d, turn_tab, turn_row, e_tab, acc, send_buf, recv_buf,
    off_ref, off_sem, d_sem, x_in, x_send, x_recv, send_sem, recv_sem, round_sem,
):
    chans, nodes = d_ref.shape
    half = own.shape[1]
    kept = own.shape[0] // chans
    group = chans // CHUNKS
    rows = kept * group
    node_rows = nodes // n_chan
    me = lax.axis_index("chan")
    tm = lax.axis_index("tm")
    partner = 1 - tm
    unit = 1.0 / SAMPLES

    rounds = n_chan.bit_length() - 1
    barrier = pltpu.get_barrier_semaphore()
    pl.semaphore_signal(barrier, inc=1, device_id={"tm": partner}, device_id_type=MESH)
    for r in range(rounds):
        pl.semaphore_signal(barrier, inc=1, device_id={"chan": flip(me, r)}, device_id_type=MESH)

    offsets_in = pltpu.make_async_copy(off_hbm, off_ref, off_sem)
    delays_in = pltpu.make_async_copy(d_hbm, d_ref, d_sem)

    def tell(r):
        if r < rounds:
            pl.semaphore_signal(round_sem.at[r], inc=1, device_id={"chan": flip(me, r)}, device_id_type=MESH)

    def hear(r):
        if r < rounds:
            pl.semaphore_wait(round_sem.at[r], 1)
            tell(r + 1)

    def mine_of(ch):
        return pltpu.make_async_copy(
            x_hbm.at[ch, pl.ds(pl.multiple_of(tm * kept, kept), kept)], own.at[pl.ds(ch * kept, kept)], x_in
        )

    def to_partner(src, dst, at):
        return pltpu.make_async_remote_copy(
            src_ref=src, dst_ref=dst, send_sem=x_send, recv_sem=x_recv.at[at],
            device_id={"tm": partner}, device_id_type=MESH,
        )

    pl.semaphore_wait(barrier, rounds + 1)
    for ch in range(chans):
        to_partner(
            x_hbm.at[ch, pl.ds(pl.multiple_of(partner * kept, kept), kept)],
            other.at[pl.ds(ch * kept, kept)], ch // group,
        ).start()
    tell(0)
    delays_in.start()
    offsets_in.start()
    for ch in range(chans):
        mine_of(ch).start()

    late = jnp.where(lax.broadcasted_iota(jnp.int32, (1, SPAN), 1) * 0 + tm == 1, -1.0, 1.0)
    residue = lax.broadcasted_iota(jnp.int32, (RADIX, SPAN), 0)
    c, s = cos_sin(residue.astype(jnp.float32) * float_iota((RADIX, SPAN), 1) * unit)
    sign = jnp.where((residue & 1) == 1, late, 1.0)
    fwd_c[...] = c * sign
    fwd_s[...] = s * sign
    inv_c[...], inv_s[...] = cos_sin(float_iota((RADIX, INNER), 0) * float_iota((RADIX, INNER), 1) * (1.0 / TIMES))
    lane = lax.broadcasted_iota(jnp.int32, (1, 2 * BINS), 1)
    quarter = jnp.where(lane < BINS, 0.0, 0.25)
    place = jnp.where(lane < BINS, lane, lane - BINS).astype(jnp.float32)
    _, s = cos_sin((RADIX * place + float_iota((RADIX, 2 * BINS), 0) + 0.5) * (0.5 / BAND))
    gain[...] = s * s * (2.0 / SAMPLES)

    def forward_table(at):
        first = pl.multiple_of(at * 32, 32)
        spot = float_iota((32, 2 * BINS), 0) + first.astype(jnp.float32)
        c, s = cos_sin(spot * ((place + BAND_LO // RADIX) * (1.0 / SPAN)) + quarter)
        for value, base in ((c, 0), (s, SPAN)):
            fwd[pl.ds(pl.multiple_of(base + first, 32), 32), :] = value.astype(jnp.bfloat16)

    pl.loop(0, SPAN // 32)(forward_table)

    row = lax.broadcasted_iota(jnp.int32, (2 * BINS, 1), 0)
    row_quarter = jnp.where(row < BINS, 0.0, 0.25)
    row_place = jnp.where(row < BINS, row, row - BINS).astype(jnp.float32)
    c, s = cos_sin(row_place * (float_iota((1, INNER), 1) * (1.0 / INNER)) + row_quarter)
    for base in (0, 2 * BINS):
        inv[0, base : base + 2 * BINS, :] = c.astype(jnp.bfloat16)
        inv[1, base : base + 2 * BINS, :] = s.astype(jnp.bfloat16)

    env_lane = lax.broadcasted_iota(jnp.int32, (1, FB), 1)
    env_place = jnp.where(env_lane < HALF_FB, env_lane, env_lane - HALF_FB).astype(jnp.float32)
    for odd in range(2):
        freq = (2.0 * env_place + (1.0 if odd else 2.0)) * (1.0 / TIMES)
        base_c, base_s = cos_sin(float_iota((32, FB), 0) * freq)
        lead_c, lead_s = cos_sin(float_iota((FOLD // 32, FB), 0) * (freq * 32.0))
        shown = (env_lane >= HALF_FB) == bool(odd)
        base_c, base_s = jnp.where(shown, base_c, 0.0), jnp.where(shown, base_s, 0.0)
        for a in range(FOLD // 32):
            lc, ls = lead_c[a : a + 1], lead_s[a : a + 1]
            at = slice(odd * FOLD + a * 32, odd * FOLD + (a + 1) * 32)
            env[0, at, :] = (lc * base_c - ls * base_s).astype(jnp.bfloat16)
            env[1, at, :] = -(ls * base_c + lc * base_s).astype(jnp.bfloat16)

    hear(0)

    delays_in.wait()
    nodes_d[...] = (d_ref[...].astype(jnp.float32) * unit).T
    bins = env_bins(1)

    def phases(step):
        at = pl.ds(pl.multiple_of(step * node_rows, node_rows), node_rows)
        delay = nodes_d[at, :]
        for ch in range(chans):
            c, s = cos_sin(delay[:, ch : ch + 1] * bins)
            phase_c[ch, at, :] = c
            phase_s[ch, at, :] = s

    def more_phases(step):
        for k in range(UNROLL):
            phases(UNROLL * step + k)

    steps = n_chan // UNROLL
    pl.loop(0, steps // 2)(more_phases)
    hear(1)
    pl.loop(steps // 2, steps)(more_phases)
    hear(2)

    turns = env_bins(0)
    c, s = cos_sin(turns * (float_iota((1, TB), 1) * (DEC * unit)))
    for first, value in ((0, c), (FB, -s)):
        for piece, part in enumerate(split(value)):
            turn_tab[first : first + FB, piece * TB : (piece + 1) * TB] = part
    offsets_in.wait()
    for w in range(kept):
        shift = off_ref[w].astype(jnp.float32) * unit
        turn_row[w, :, :FB], turn_row[w, :, FB:] = cos_sin(bins * shift)

    pltpu.make_async_copy(own, own, x_in).wait()

    def residues(at):
        mine = own[at, :].astype(jnp.float32)
        theirs = other[at, :].astype(jnp.float32)
        a, b = [], []
        for q in range(RADIX // 2):
            cols = slice(q * SPAN, (q + 1) * SPAN)
            a.append(mine[:, cols] + theirs[:, cols])
            b.append(mine[:, cols] - theirs[:, cols])
        s02, d02, s13, d13 = a[0] + a[2], a[0] - a[2], a[1] + a[3], a[1] - a[3]
        t, u = (b[1] - b[3]) * root_half, (b[1] + b[3]) * root_half
        one = (b[0] + t, -(u + b[2]))
        three = (b[0] - t, b[2] - u)
        parts = [
            (s02 + s13, None), one, (d02, -d13), three,
            (s02 - s13, None), (three[0], -three[1]), (d02, d13), (one[0], -one[1]),
        ]
        stacked = []
        for r in ORDER:
            re, im = parts[r]
            if r == 0:
                zr, zi = re, jnp.zeros_like(re)
            else:
                c, s = fwd_c[r : r + 1, :], fwd_s[r : r + 1, :]
                if im is None:
                    zr, zi = re * c, -(re * s)
                else:
                    zr, zi = re * c + im * s, im * c - re * s
            stacked.append(jnp.concatenate([zr, zi], axis=1).astype(jnp.bfloat16))
        return stacked

    def energies(inner):
        turned = [None] * RADIX
        for i, r in enumerate(ORDER):
            re, im = inner[i * TILE : (i + 1) * TILE, :INNER], inner[i * TILE : (i + 1) * TILE, INNER:]
            if r:
                c, s = inv_c[r : r + 1, :], inv_s[r : r + 1, :]
                re, im = re * c - im * s, re * s + im * c
            turned[r] = (re, im)
        evens, odds = inverse_four(turned[0::2]), inverse_four(turned[1::2])
        same, cross = [], []
        for q in range(RADIX // 2):
            (er, ei), (fr, fi) = evens[q], odds[q]
            same.append((er * er + ei * ei) + (fr * fr + fi * fi))
            if q == 0:
                both = 2.0 * (er * fr + ei * fi)
            elif q == 1:
                both = (2.0 * root_half) * (er * (fr - fi) + ei * (fr + fi))
            elif q == 2:
                both = 2.0 * (ei * fr - er * fi)
            else:
                both = (2.0 * root_half) * (ei * (fr - fi) - er * (fr + fi))
            cross.append(both)
        total = jnp.sum((same[0] + same[1]) + (same[2] + same[3]), axis=1, keepdims=True)
        factor = 4.0 / (math.sqrt(SAMPLES) * (total * (4.0 / SAMPLES) + epsilon))
        return jnp.concatenate(same + cross, axis=1).astype(jnp.bfloat16), factor

    def envelope(g):
        tiles = rows // TILE
        stacked = []
        for h in range(tiles):
            stacked += residues(pl.ds(pl.multiple_of(g * rows + h * TILE, TILE), TILE))
        spectrum = jnp.dot(jnp.concatenate(stacked, axis=0), fwd[...], preferred_element_type=jnp.float32)
        tapered = []
        for i in range(tiles * RADIX):
            r = ORDER[i % RADIX]
            high, low = split(spectrum[i * TILE : (i + 1) * TILE] * gain[r : r + 1, :])
            tapered.append(jnp.concatenate([high, low], axis=1))
        inner = jnp.dot(
            jnp.concatenate(tapered, axis=0), jnp.concatenate([inv[0], inv[1]], axis=1),
            preferred_element_type=jnp.float32,
        )
        found = [energies(inner[h * RADIX * TILE : (h + 1) * RADIX * TILE]) for h in range(tiles)]
        spread = jnp.dot(
            jnp.concatenate([energy for energy, _ in found], axis=0),
            jnp.concatenate([env[0], env[1]], axis=1), preferred_element_type=jnp.float32,
        )
        for h in range(tiles):
            e_tab[g, h * TILE : (h + 1) * TILE, :] = spread[h * TILE : (h + 1) * TILE] * found[h][1]

    def outgoing(dest):
        return pltpu.make_async_remote_copy(
            src_ref=send_buf.at[dest],
            dst_ref=recv_buf.at[me],
            send_sem=send_sem,
            recv_sem=recv_sem.at[me],
            device_id={"chan": dest},
            device_id_type=MESH,
        )

    def send(dest):
        @pl.when(dest != me)
        def _():
            outgoing(dest).start()

    def stack_up(g, dest, sums):
        at = pl.ds(pl.multiple_of(dest * node_rows, node_rows), node_rows)
        for ch in range(group):
            pc = phase_c[g * group + ch, at, :]
            ps = phase_s[g * group + ch, at, :]
            for w in range(kept):
                r = kept * ch + w
                er, ei = e_tab[g, r : r + 1, :FB], e_tab[g, r : r + 1, FB:]
                sums[0][w] = sums[0][w] + (pc * er - ps * ei)
                sums[1][w] = sums[1][w] + (pc * ei + ps * er)
        return sums

    def pack(dest, sums):
        packed = jnp.concatenate([sums[p][w] for p in range(2) for w in range(kept)], axis=0)
        send_buf[dest] = packed.astype(jnp.bfloat16)

    acc[...] = jnp.zeros_like(acc)

    @pl.loop(0, CHUNKS)
    def _(g):
        arrived = other.at[pl.ds(pl.multiple_of(g * rows, rows), rows)]
        to_partner(arrived, arrived, g).wait_recv()
        envelope(g)
        for step in range(EARLY):
            sums = stack_up(g, step, [[acc[step, p * kept + w] for w in range(kept)] for p in range(2)])
            for p in range(2):
                for w in range(kept):
                    acc[step, p * kept + w] = sums[p][w]

            @pl.when(g == CHUNKS - 1)
            def _():
                pack(step, sums)
                if step == 1:
                    for r in range(3, rounds):
                        hear(r)
                if step:
                    send(step - 1)

    @pl.loop(EARLY, n_chan)
    def _(step):
        sums = [[jnp.zeros((node_rows, FB), jnp.float32) for _ in range(kept)] for _ in range(2)]
        for g in range(CHUNKS):
            sums = stack_up(g, step, sums)
        pack(step, sums)
        send(step - 1)

    send(n_chan - 1)

    def incoming(source):
        return pltpu.make_async_remote_copy(
            src_ref=send_buf.at[source],
            dst_ref=recv_buf.at[source],
            send_sem=send_sem,
            recv_sem=recv_sem.at[source],
            device_id={"chan": source},
            device_id_type=MESH,
        )

    def add_one(step, stack):
        source = lax.rem(me + step, n_chan)
        incoming(source).wait_recv()
        return stack + recv_buf[source].astype(jnp.float32)

    stack = lax.fori_loop(1, n_chan, add_one, send_buf[me].astype(jnp.float32))

    turned = []
    for w in range(kept):
        c, s = turn_row[w, :, :FB], turn_row[w, :, FB:]
        re = stack[w * node_rows : (w + 1) * node_rows]
        im = stack[(kept + w) * node_rows : (kept + w + 1) * node_rows]
        turned.append(jnp.concatenate([re * c - im * s, re * s + im * c], axis=1))
    high, low = split(jnp.concatenate(turned, axis=0))
    bright = jnp.dot(
        jnp.concatenate([high, low], axis=0), turn_tab[...], preferred_element_type=jnp.float32
    )
    size = kept * node_rows
    bright = bright[:size, :TB] + (bright[:size, TB:] + bright[size:, :TB])
    scale = 1.0 / math.sqrt(FB * chans * n_chan)
    out_ref[...] = (bright * scale).reshape(kept, node_rows, TB)

    to_partner(other, other, 0).wait_send()
    pltpu.make_async_remote_copy(
        src_ref=send_buf.at[pl.ds(0, n_chan - 1)],
        dst_ref=recv_buf.at[pl.ds(0, n_chan - 1)],
        send_sem=send_sem,
        recv_sem=recv_sem.at[0],
        device_id={"chan": flip(me, 0)},
        device_id_type=MESH,
    ).wait_send()


def solution(mesh):
    n_chan = mesh.shape["chan"]

    def on_device(traces, delays, offsets):
        chans, windows, half = traces.shape
        nodes = delays.shape[0]
        kept = offsets.shape[0]
        node_rows = nodes // n_chan
        packed_rows = 2 * kept * node_rows
        hbm = pl.BlockSpec(memory_space=pltpu.HBM)
        return pl.pallas_call(
            functools.partial(kernel, n_chan),
            out_shape=jax.ShapeDtypeStruct((kept, node_rows, TB), jnp.float32),
            in_specs=[hbm] * 3,
            out_specs=pl.BlockSpec(memory_space=pltpu.VMEM),
            scratch_shapes=[
                pltpu.VMEM((chans, nodes), jnp.int32),
                pltpu.VMEM((chans * kept, half), jnp.bfloat16),
                pltpu.VMEM((chans * kept, half), jnp.bfloat16),
                pltpu.VMEM((2 * SPAN, 2 * BINS), jnp.bfloat16),
                pltpu.VMEM((2, 4 * BINS, INNER), jnp.bfloat16),
                pltpu.VMEM((2, TIMES, FB), jnp.bfloat16),
                pltpu.VMEM((RADIX, SPAN), jnp.float32),
                pltpu.VMEM((RADIX, SPAN), jnp.float32),
                pltpu.VMEM((RADIX, INNER), jnp.float32),
                pltpu.VMEM((RADIX, INNER), jnp.float32),
                pltpu.VMEM((RADIX, 2 * BINS), jnp.float32),
                pltpu.VMEM((chans, nodes, FB), jnp.float32),
                pltpu.VMEM((chans, nodes, FB), jnp.float32),
                pltpu.VMEM((nodes, chans), jnp.float32),
                pltpu.VMEM((2 * FB, 2 * TB), jnp.bfloat16),
                pltpu.VMEM((kept, 1, 2 * FB), jnp.float32),
                pltpu.VMEM((CHUNKS, kept * chans // CHUNKS, 2 * FB), jnp.float32),
                pltpu.VMEM((EARLY, 2 * kept, node_rows, FB), jnp.float32),
                pltpu.VMEM((n_chan, packed_rows, FB), jnp.bfloat16),
                pltpu.VMEM((n_chan, packed_rows, FB), jnp.bfloat16),
                pltpu.SMEM((kept,), jnp.int32),
                pltpu.SemaphoreType.DMA,
                pltpu.SemaphoreType.DMA,
                pltpu.SemaphoreType.DMA,
                pltpu.SemaphoreType.DMA,
                pltpu.SemaphoreType.DMA((CHUNKS,)),
                pltpu.SemaphoreType.DMA,
                pltpu.SemaphoreType.DMA((n_chan,)),
                pltpu.SemaphoreType.REGULAR((n_chan.bit_length() - 1,)),
            ],
            compiler_params=pltpu.CompilerParams(
                collective_id=0, has_side_effects=True, vmem_limit_bytes=16 * 1024 * 1024 + 8 * chans * nodes * FB
            ),
        )(*(pltpu.with_memory_space_constraint(a, pltpu.HBM) for a in (traces, delays.T, offsets)))

    placed = (P("chan", None, "tm"), P(None, "chan"), P("tm"))
    return jax.shard_map(
        on_device, mesh=mesh, in_specs=placed, out_specs=P("tm", "chan", None), check_vma=False
    )
```

```python
import functools
import math

import jax
import jax.numpy as jnp
from jax import lax
from jax.experimental import pallas as pl
from jax.experimental.pallas import tpu as pltpu
from jax.sharding import PartitionSpec as P

SAMPLES = 2048
BAND = 512
FB = 128
TB = 256
BAND_LO = 128
DEC = 8
UNROLL = 4
CHUNKS = 2
EARLY = 2

RADIX = 8
ORDER = (0, 4, 2, 6, 1, 5, 3, 7)
TILE = 16
SPAN = SAMPLES // RADIX
BINS = BAND // RADIX
TIMES = SAMPLES // 2
FOLD = TIMES // 2
INNER = TIMES // RADIX
HALF_FB = FB // 2

epsilon = 1e-06
full_turn = 2.0 * math.pi
root_half = math.sqrt(0.5)
MESH = pl.DeviceIdType.MESH


COS_HALF = (
    1.4142134965650053, -6.978850988237948, 5.73946117066148, -1.8835629871727047, 0.3106981915530425,
)
SIN_HALF = (
    4.442882834149914, -7.30824115454536, 3.6062889582107696, -0.845763596066154, 0.10920575349257165,
)


def cos_sin(turns):
    x = turns - jnp.round(turns)
    y = x * x
    c, s = COS_HALF[-1], SIN_HALF[-1]
    for c_next, s_next in zip(COS_HALF[-2::-1], SIN_HALF[-2::-1]):
        c = c * y + c_next
        s = s * y + s_next
    return c * c - 1.0, s * x * c


def float_iota(shape, axis):
    return lax.broadcasted_iota(jnp.int32, shape, axis).astype(jnp.float32)


def bit_of(value, at):
    return lax.rem(value // (1 << at), 2)


def flip(value, at):
    return value ^ (1 << at)


def split(value):
    high = value.astype(jnp.bfloat16)
    return high, (value - high.astype(jnp.float32)).astype(jnp.bfloat16)


def env_bins(axis):
    shape = (1, FB) if axis else (FB, 1)
    lane = lax.broadcasted_iota(jnp.int32, shape, axis)
    return jnp.where(lane < HALF_FB, 2 * lane + 2, 2 * lane - (FB - 1)).astype(jnp.float32)


def inverse_four(values):
    (ar, ai), (br, bi), (cr, ci), (dr, di) = values
    sr, si, er, ei = ar + cr, ai + ci, ar - cr, ai - ci
    tr, ti, fr, fi = br + dr, bi + di, br - dr, bi - di
    return [(sr + tr, si + ti), (er - fi, ei + fr), (sr - tr, si - ti), (er + fi, ei - fr)]


def kernel(
    n_chan, x_hbm, d_hbm, off_hbm, out_ref,
    d_ref, own, other, fwd, inv, env, fwd_c, fwd_s, inv_c, inv_s, gain, phase_c, phase_s,
    nodes_d, turn_tab, turn_row, e_tab, acc, send_buf, recv_buf,
    off_ref, off_sem, d_sem, x_in, x_send, x_recv, send_sem, recv_sem, round_sem,
):
    chans, nodes = d_ref.shape
    half = own.shape[1]
    kept = own.shape[0] // chans
    group = chans // CHUNKS
    rows = kept * group
    node_rows = nodes // n_chan
    me = lax.axis_index("chan")
    tm = lax.axis_index("tm")
    partner = 1 - tm
    unit = 1.0 / SAMPLES

    rounds = n_chan.bit_length() - 1
    barrier = pltpu.get_barrier_semaphore()
    pl.semaphore_signal(barrier, inc=1, device_id={"tm": partner}, device_id_type=MESH)
    for r in range(rounds):
        pl.semaphore_signal(barrier, inc=1, device_id={"chan": flip(me, r)}, device_id_type=MESH)

    offsets_in = pltpu.make_async_copy(off_hbm, off_ref, off_sem)
    delays_in = pltpu.make_async_copy(d_hbm, d_ref, d_sem)

    def tell(r):
        if r < rounds:
            pl.semaphore_signal(round_sem.at[r], inc=1, device_id={"chan": flip(me, r)}, device_id_type=MESH)

    def hear(r):
        if r < rounds:
            pl.semaphore_wait(round_sem.at[r], 1)
            tell(r + 1)

    def mine_of(ch):
        return pltpu.make_async_copy(
            x_hbm.at[ch, pl.ds(pl.multiple_of(tm * kept, kept), kept)], own.at[pl.ds(ch * kept, kept)], x_in
        )

    def to_partner(src, dst, at):
        return pltpu.make_async_remote_copy(
            src_ref=src, dst_ref=dst, send_sem=x_send, recv_sem=x_recv.at[at],
            device_id={"tm": partner}, device_id_type=MESH,
        )

    pl.semaphore_wait(barrier, rounds + 1)
    for ch in range(chans):
        to_partner(
            x_hbm.at[ch, pl.ds(pl.multiple_of(partner * kept, kept), kept)],
            other.at[pl.ds(ch * kept, kept)], ch // group,
        ).start()
    tell(0)
    delays_in.start()
    offsets_in.start()
    for ch in range(chans):
        mine_of(ch).start()

    late = jnp.where(lax.broadcasted_iota(jnp.int32, (1, SPAN), 1) * 0 + tm == 1, -1.0, 1.0)
    residue = lax.broadcasted_iota(jnp.int32, (RADIX, SPAN), 0)
    c, s = cos_sin(residue.astype(jnp.float32) * float_iota((RADIX, SPAN), 1) * unit)
    sign = jnp.where((residue & 1) == 1, late, 1.0)
    fwd_c[...] = c * sign
    fwd_s[...] = s * sign
    inv_c[...], inv_s[...] = cos_sin(float_iota((RADIX, INNER), 0) * float_iota((RADIX, INNER), 1) * (1.0 / TIMES))
    lane = lax.broadcasted_iota(jnp.int32, (1, 2 * BINS), 1)
    quarter = jnp.where(lane < BINS, 0.0, 0.25)
    place = jnp.where(lane < BINS, lane, lane - BINS).astype(jnp.float32)
    _, s = cos_sin((RADIX * place + float_iota((RADIX, 2 * BINS), 0) + 0.5) * (0.5 / BAND))
    gain[...] = s * s * (2.0 / SAMPLES)

    def forward_table(at):
        first = pl.multiple_of(at * 32, 32)
        spot = float_iota((32, 2 * BINS), 0) + first.astype(jnp.float32)
        c, s = cos_sin(spot * ((place + BAND_LO // RADIX) * (1.0 / SPAN)) + quarter)
        for value, base in ((c, 0), (s, SPAN)):
            fwd[pl.ds(pl.multiple_of(base + first, 32), 32), :] = value.astype(jnp.bfloat16)

    pl.loop(0, SPAN // 32)(forward_table)

    row = lax.broadcasted_iota(jnp.int32, (2 * BINS, 1), 0)
    row_quarter = jnp.where(row < BINS, 0.0, 0.25)
    row_place = jnp.where(row < BINS, row, row - BINS).astype(jnp.float32)
    c, s = cos_sin(row_place * (float_iota((1, INNER), 1) * (1.0 / INNER)) + row_quarter)
    for base in (0, 2 * BINS):
        inv[0, base : base + 2 * BINS, :] = c.astype(jnp.bfloat16)
        inv[1, base : base + 2 * BINS, :] = s.astype(jnp.bfloat16)

    env_lane = lax.broadcasted_iota(jnp.int32, (1, FB), 1)
    env_place = jnp.where(env_lane < HALF_FB, env_lane, env_lane - HALF_FB).astype(jnp.float32)
    for odd in range(2):
        freq = (2.0 * env_place + (1.0 if odd else 2.0)) * (1.0 / TIMES)
        base_c, base_s = cos_sin(float_iota((32, FB), 0) * freq)
        lead_c, lead_s = cos_sin(float_iota((FOLD // 32, FB), 0) * (freq * 32.0))
        shown = (env_lane >= HALF_FB) == bool(odd)
        base_c, base_s = jnp.where(shown, base_c, 0.0), jnp.where(shown, base_s, 0.0)
        for a in range(FOLD // 32):
            lc, ls = lead_c[a : a + 1], lead_s[a : a + 1]
            at = slice(odd * FOLD + a * 32, odd * FOLD + (a + 1) * 32)
            env[0, at, :] = (lc * base_c - ls * base_s).astype(jnp.bfloat16)
            env[1, at, :] = -(ls * base_c + lc * base_s).astype(jnp.bfloat16)

    hear(0)

    delays_in.wait()
    nodes_d[...] = (d_ref[...].astype(jnp.float32) * unit).T
    bins = env_bins(1)

    def phases(step):
        at = pl.ds(pl.multiple_of(step * node_rows, node_rows), node_rows)
        delay = nodes_d[at, :]
        for ch in range(chans):
            c, s = cos_sin(delay[:, ch : ch + 1] * bins)
            phase_c[ch, at, :] = c
            phase_s[ch, at, :] = s

    def more_phases(step):
        for k in range(UNROLL):
            phases(UNROLL * step + k)

    steps = n_chan // UNROLL
    pl.loop(0, steps // 2)(more_phases)
    hear(1)
    pl.loop(steps // 2, steps)(more_phases)
    hear(2)

    turns = env_bins(0)
    c, s = cos_sin(turns * (float_iota((1, TB), 1) * (DEC * unit)))
    for first, value in ((0, c), (FB, -s)):
        for piece, part in enumerate(split(value)):
            turn_tab[first : first + FB, piece * TB : (piece + 1) * TB] = part
    offsets_in.wait()
    for w in range(kept):
        shift = off_ref[w].astype(jnp.float32) * unit
        turn_row[w, :, :FB], turn_row[w, :, FB:] = cos_sin(bins * shift)

    pltpu.make_async_copy(own, own, x_in).wait()

    def residues(at):
        mine = own[at, :].astype(jnp.float32)
        theirs = other[at, :].astype(jnp.float32)
        a, b = [], []
        for q in range(RADIX // 2):
            cols = slice(q * SPAN, (q + 1) * SPAN)
            a.append(mine[:, cols] + theirs[:, cols])
            b.append(mine[:, cols] - theirs[:, cols])
        s02, d02, s13, d13 = a[0] + a[2], a[0] - a[2], a[1] + a[3], a[1] - a[3]
        t, u = (b[1] - b[3]) * root_half, (b[1] + b[3]) * root_half
        one = (b[0] + t, -(u + b[2]))
        three = (b[0] - t, b[2] - u)
        parts = [
            (s02 + s13, None), one, (d02, -d13), three,
            (s02 - s13, None), (three[0], -three[1]), (d02, d13), (one[0], -one[1]),
        ]
        stacked = []
        for r in ORDER:
            re, im = parts[r]
            if r == 0:
                zr, zi = re, jnp.zeros_like(re)
            else:
                c, s = fwd_c[r : r + 1, :], fwd_s[r : r + 1, :]
                if im is None:
                    zr, zi = re * c, -(re * s)
                else:
                    zr, zi = re * c + im * s, im * c - re * s
            stacked.append(jnp.concatenate([zr, zi], axis=1).astype(jnp.bfloat16))
        return stacked

    def energies(inner):
        turned = [None] * RADIX
        for i, r in enumerate(ORDER):
            re, im = inner[i * TILE : (i + 1) * TILE, :INNER], inner[i * TILE : (i + 1) * TILE, INNER:]
            if r:
                c, s = inv_c[r : r + 1, :], inv_s[r : r + 1, :]
                re, im = re * c - im * s, re * s + im * c
            turned[r] = (re, im)
        evens, odds = inverse_four(turned[0::2]), inverse_four(turned[1::2])
        same, cross = [], []
        for q in range(RADIX // 2):
            (er, ei), (fr, fi) = evens[q], odds[q]
            same.append((er * er + ei * ei) + (fr * fr + fi * fi))
            if q == 0:
                both = 2.0 * (er * fr + ei * fi)
            elif q == 1:
                both = (2.0 * root_half) * (er * (fr - fi) + ei * (fr + fi))
            elif q == 2:
                both = 2.0 * (ei * fr - er * fi)
            else:
                both = (2.0 * root_half) * (ei * (fr - fi) - er * (fr + fi))
            cross.append(both)
        total = jnp.sum((same[0] + same[1]) + (same[2] + same[3]), axis=1, keepdims=True)
        factor = 4.0 / (math.sqrt(SAMPLES) * (total * (4.0 / SAMPLES) + epsilon))
        return jnp.concatenate(same + cross, axis=1).astype(jnp.bfloat16), factor

    def envelope(g):
        tiles = rows // TILE
        stacked = []
        for h in range(tiles):
            stacked += residues(pl.ds(pl.multiple_of(g * rows + h * TILE, TILE), TILE))
        spectrum = jnp.dot(jnp.concatenate(stacked, axis=0), fwd[...], preferred_element_type=jnp.float32)
        tapered = []
        for i in range(tiles * RADIX):
            r = ORDER[i % RADIX]
            high, low = split(spectrum[i * TILE : (i + 1) * TILE] * gain[r : r + 1, :])
            tapered.append(jnp.concatenate([high, low], axis=1))
        inner = jnp.dot(
            jnp.concatenate(tapered, axis=0), jnp.concatenate([inv[0], inv[1]], axis=1),
            preferred_element_type=jnp.float32,
        )
        found = [energies(inner[h * RADIX * TILE : (h + 1) * RADIX * TILE]) for h in range(tiles)]
        spread = jnp.dot(
            jnp.concatenate([energy for energy, _ in found], axis=0),
            jnp.concatenate([env[0], env[1]], axis=1), preferred_element_type=jnp.float32,
        )
        for h in range(tiles):
            e_tab[g, h * TILE : (h + 1) * TILE, :] = spread[h * TILE : (h + 1) * TILE] * found[h][1]

    def outgoing(dest):
        return pltpu.make_async_remote_copy(
            src_ref=send_buf.at[dest],
            dst_ref=recv_buf.at[me],
            send_sem=send_sem,
            recv_sem=recv_sem.at[me],
            device_id={"chan": dest},
            device_id_type=MESH,
        )

    def send(dest):
        @pl.when(dest != me)
        def _():
            outgoing(dest).start()

    def stack_up(g, dest, sums):
        at = pl.ds(pl.multiple_of(dest * node_rows, node_rows), node_rows)
        for ch in range(group):
            pc = phase_c[g * group + ch, at, :]
            ps = phase_s[g * group + ch, at, :]
            for w in range(kept):
                r = kept * ch + w
                er, ei = e_tab[g, r : r + 1, :FB], e_tab[g, r : r + 1, FB:]
                sums[0][w] = sums[0][w] + (pc * er - ps * ei)
                sums[1][w] = sums[1][w] + (pc * ei + ps * er)
        return sums

    def pack(dest, sums):
        packed = jnp.concatenate([sums[p][w] for p in range(2) for w in range(kept)], axis=0)
        send_buf[dest] = packed.astype(jnp.bfloat16)

    acc[...] = jnp.zeros_like(acc)

    @pl.loop(0, CHUNKS)
    def _(g):
        arrived = other.at[pl.ds(pl.multiple_of(g * rows, rows), rows)]
        to_partner(arrived, arrived, g).wait_recv()
        envelope(g)
        for step in range(EARLY):
            sums = stack_up(g, step, [[acc[step, p * kept + w] for w in range(kept)] for p in range(2)])
            for p in range(2):
                for w in range(kept):
                    acc[step, p * kept + w] = sums[p][w]

            pack(step, sums)
            if step:
                @pl.when(g == CHUNKS - 1)
                def _():
                    if step == 1:
                        for r in range(3, rounds):
                            hear(r)
                    send(step - 1)

    @pl.loop(EARLY, n_chan)
    def _(step):
        sums = [[jnp.zeros((node_rows, FB), jnp.float32) for _ in range(kept)] for _ in range(2)]
        for g in range(CHUNKS):
            sums = stack_up(g, step, sums)
        pack(step, sums)
        send(step - 1)

    send(n_chan - 1)

    def incoming(source):
        return pltpu.make_async_remote_copy(
            src_ref=send_buf.at[source],
            dst_ref=recv_buf.at[source],
            send_sem=send_sem,
            recv_sem=recv_sem.at[source],
            device_id={"chan": source},
            device_id_type=MESH,
        )

    def add_one(step, stack):
        source = lax.rem(me + step, n_chan)
        incoming(source).wait_recv()
        return stack + recv_buf[source].astype(jnp.float32)

    stack = lax.fori_loop(1, n_chan, add_one, send_buf[me].astype(jnp.float32))

    turned = []
    for w in range(kept):
        c, s = turn_row[w, :, :FB], turn_row[w, :, FB:]
        re = stack[w * node_rows : (w + 1) * node_rows]
        im = stack[(kept + w) * node_rows : (kept + w + 1) * node_rows]
        turned.append(jnp.concatenate([re * c - im * s, re * s + im * c], axis=1))
    high, low = split(jnp.concatenate(turned, axis=0))
    bright = jnp.dot(
        jnp.concatenate([high, low], axis=0), turn_tab[...], preferred_element_type=jnp.float32
    )
    size = kept * node_rows
    bright = bright[:size, :TB] + (bright[:size, TB:] + bright[size:, :TB])
    scale = 1.0 / math.sqrt(FB * chans * n_chan)
    out_ref[...] = (bright * scale).reshape(kept, node_rows, TB)

    to_partner(other, other, 0).wait_send()
    pltpu.make_async_remote_copy(
        src_ref=send_buf.at[pl.ds(0, n_chan - 1)],
        dst_ref=recv_buf.at[pl.ds(0, n_chan - 1)],
        send_sem=send_sem,
        recv_sem=recv_sem.at[0],
        device_id={"chan": flip(me, 0)},
        device_id_type=MESH,
    ).wait_send()


def solution(mesh):
    n_chan = mesh.shape["chan"]

    def on_device(traces, delays, offsets):
        chans, windows, half = traces.shape
        nodes = delays.shape[0]
        kept = offsets.shape[0]
        node_rows = nodes // n_chan
        packed_rows = 2 * kept * node_rows
        hbm = pl.BlockSpec(memory_space=pltpu.HBM)
        return pl.pallas_call(
            functools.partial(kernel, n_chan),
            out_shape=jax.ShapeDtypeStruct((kept, node_rows, TB), jnp.float32),
            in_specs=[hbm] * 3,
            out_specs=pl.BlockSpec(memory_space=pltpu.VMEM),
            scratch_shapes=[
                pltpu.VMEM((chans, nodes), jnp.int32),
                pltpu.VMEM((chans * kept, half), jnp.bfloat16),
                pltpu.VMEM((chans * kept, half), jnp.bfloat16),
                pltpu.VMEM((2 * SPAN, 2 * BINS), jnp.bfloat16),
                pltpu.VMEM((2, 4 * BINS, INNER), jnp.bfloat16),
                pltpu.VMEM((2, TIMES, FB), jnp.bfloat16),
                pltpu.VMEM((RADIX, SPAN), jnp.float32),
                pltpu.VMEM((RADIX, SPAN), jnp.float32),
                pltpu.VMEM((RADIX, INNER), jnp.float32),
                pltpu.VMEM((RADIX, INNER), jnp.float32),
                pltpu.VMEM((RADIX, 2 * BINS), jnp.float32),
                pltpu.VMEM((chans, nodes, FB), jnp.float32),
                pltpu.VMEM((chans, nodes, FB), jnp.float32),
                pltpu.VMEM((nodes, chans), jnp.float32),
                pltpu.VMEM((2 * FB, 2 * TB), jnp.bfloat16),
                pltpu.VMEM((kept, 1, 2 * FB), jnp.float32),
                pltpu.VMEM((CHUNKS, kept * chans // CHUNKS, 2 * FB), jnp.float32),
                pltpu.VMEM((EARLY, 2 * kept, node_rows, FB), jnp.float32),
                pltpu.VMEM((n_chan, packed_rows, FB), jnp.bfloat16),
                pltpu.VMEM((n_chan, packed_rows, FB), jnp.bfloat16),
                pltpu.SMEM((kept,), jnp.int32),
                pltpu.SemaphoreType.DMA,
                pltpu.SemaphoreType.DMA,
                pltpu.SemaphoreType.DMA,
                pltpu.SemaphoreType.DMA,
                pltpu.SemaphoreType.DMA((CHUNKS,)),
                pltpu.SemaphoreType.DMA,
                pltpu.SemaphoreType.DMA((n_chan,)),
                pltpu.SemaphoreType.REGULAR((n_chan.bit_length() - 1,)),
            ],
            compiler_params=pltpu.CompilerParams(
                collective_id=0, has_side_effects=True, vmem_limit_bytes=16 * 1024 * 1024 + 8 * chans * nodes * FB
            ),
        )(*(pltpu.with_memory_space_constraint(a, pltpu.HBM) for a in (traces, delays.T, offsets)))

    placed = (P("chan", None, "tm"), P(None, "chan"), P("tm"))
    return jax.shard_map(
        on_device, mesh=mesh, in_specs=placed, out_specs=P("tm", "chan", None), check_vma=False
    )
```

```python
import functools
import math

import jax
import jax.numpy as jnp
from jax import lax
from jax.experimental import pallas as pl
from jax.experimental.pallas import tpu as pltpu
from jax.sharding import PartitionSpec as P

SAMPLES = 2048
BAND = 512
FB = 128
TB = 256
BAND_LO = 128
DEC = 8
UNROLL = 4
CHUNKS = 2
EARLY = 2

RADIX = 8
ORDER = (0, 4, 2, 6, 1, 5, 3, 7)
TILE = 16
SPAN = SAMPLES // RADIX
BINS = BAND // RADIX
TIMES = SAMPLES // 2
FOLD = TIMES // 2
INNER = TIMES // RADIX
HALF_FB = FB // 2

epsilon = 1e-06
full_turn = 2.0 * math.pi
root_half = math.sqrt(0.5)
MESH = pl.DeviceIdType.MESH


COS_HALF = (
    1.4142134965650053, -6.978850988237948, 5.73946117066148, -1.8835629871727047, 0.3106981915530425,
)
SIN_HALF = (
    4.442882834149914, -7.30824115454536, 3.6062889582107696, -0.845763596066154, 0.10920575349257165,
)


def cos_sin(turns):
    x = turns - jnp.round(turns)
    y = x * x
    c, s = COS_HALF[-1], SIN_HALF[-1]
    for c_next, s_next in zip(COS_HALF[-2::-1], SIN_HALF[-2::-1]):
        c = c * y + c_next
        s = s * y + s_next
    return c * c - 1.0, s * x * c


def float_iota(shape, axis):
    return lax.broadcasted_iota(jnp.int32, shape, axis).astype(jnp.float32)


def bit_of(value, at):
    return lax.rem(value // (1 << at), 2)


def flip(value, at):
    return value ^ (1 << at)


def split(value):
    high = value.astype(jnp.bfloat16)
    return high, (value - high.astype(jnp.float32)).astype(jnp.bfloat16)


def env_bins(axis):
    shape = (1, FB) if axis else (FB, 1)
    lane = lax.broadcasted_iota(jnp.int32, shape, axis)
    return jnp.where(lane < HALF_FB, 2 * lane + 2, 2 * lane - (FB - 1)).astype(jnp.float32)


def inverse_four(values):
    (ar, ai), (br, bi), (cr, ci), (dr, di) = values
    sr, si, er, ei = ar + cr, ai + ci, ar - cr, ai - ci
    tr, ti, fr, fi = br + dr, bi + di, br - dr, bi - di
    return [(sr + tr, si + ti), (er - fi, ei + fr), (sr - tr, si - ti), (er + fi, ei - fr)]


def kernel(
    n_chan, x_hbm, d_hbm, off_hbm, out_ref,
    d_ref, own, other, fwd, inv, env, fwd_c, fwd_s, inv_c, inv_s, gain, phase_c, phase_s,
    nodes_d, turn_tab, turn_row, e_tab, acc, send_buf, recv_buf,
    off_ref, off_sem, d_sem, x_in, x_send, x_recv, send_sem, recv_sem, round_sem,
):
    chans, nodes = d_ref.shape
    half = own.shape[1]
    kept = own.shape[0] // chans
    group = chans // CHUNKS
    rows = kept * group
    node_rows = nodes // n_chan
    me = lax.axis_index("chan")
    tm = lax.axis_index("tm")
    partner = 1 - tm
    unit = 1.0 / SAMPLES

    rounds = n_chan.bit_length() - 1
    barrier = pltpu.get_barrier_semaphore()
    pl.semaphore_signal(barrier, inc=1, device_id={"tm": partner}, device_id_type=MESH)
    for r in range(rounds):
        pl.semaphore_signal(barrier, inc=1, device_id={"chan": flip(me, r)}, device_id_type=MESH)

    offsets_in = pltpu.make_async_copy(off_hbm, off_ref, off_sem)
    delays_in = pltpu.make_async_copy(d_hbm, d_ref, d_sem)

    def tell(r):
        if r < rounds:
            pl.semaphore_signal(round_sem.at[r], inc=1, device_id={"chan": flip(me, r)}, device_id_type=MESH)

    def hear(r):
        if r < rounds:
            pl.semaphore_wait(round_sem.at[r], 1)
            tell(r + 1)

    def mine_of(ch):
        return pltpu.make_async_copy(
            x_hbm.at[ch, pl.ds(pl.multiple_of(tm * kept, kept), kept)], own.at[pl.ds(ch * kept, kept)], x_in
        )

    def to_partner(src, dst, at):
        return pltpu.make_async_remote_copy(
            src_ref=src, dst_ref=dst, send_sem=x_send, recv_sem=x_recv.at[at],
            device_id={"tm": partner}, device_id_type=MESH,
        )

    pl.semaphore_wait(barrier, rounds + 1)
    for ch in range(chans):
        to_partner(
            x_hbm.at[ch, pl.ds(pl.multiple_of(partner * kept, kept), kept)],
            other.at[pl.ds(ch * kept, kept)], ch // group,
        ).start()
    tell(0)
    delays_in.start()
    offsets_in.start()
    for ch in range(chans):
        mine_of(ch).start()

    late = jnp.where(lax.broadcasted_iota(jnp.int32, (1, SPAN), 1) * 0 + tm == 1, -1.0, 1.0)
    residue = lax.broadcasted_iota(jnp.int32, (RADIX, SPAN), 0)
    c, s = cos_sin(residue.astype(jnp.float32) * float_iota((RADIX, SPAN), 1) * unit)
    sign = jnp.where((residue & 1) == 1, late, 1.0)
    fwd_c[...] = c * sign
    fwd_s[...] = s * sign
    inv_c[...], inv_s[...] = cos_sin(float_iota((RADIX, INNER), 0) * float_iota((RADIX, INNER), 1) * (1.0 / TIMES))
    lane = lax.broadcasted_iota(jnp.int32, (1, 2 * BINS), 1)
    quarter = jnp.where(lane < BINS, 0.0, 0.25)
    place = jnp.where(lane < BINS, lane, lane - BINS).astype(jnp.float32)
    _, s = cos_sin((RADIX * place + float_iota((RADIX, 2 * BINS), 0) + 0.5) * (0.5 / BAND))
    gain[...] = s * s * (2.0 / SAMPLES)

    def forward_table(at):
        first = pl.multiple_of(at * 32, 32)
        spot = float_iota((32, 2 * BINS), 0) + first.astype(jnp.float32)
        c, s = cos_sin(spot * ((place + BAND_LO // RADIX) * (1.0 / SPAN)) + quarter)
        for value, base in ((c, 0), (s, SPAN)):
            fwd[pl.ds(pl.multiple_of(base + first, 32), 32), :] = value.astype(jnp.bfloat16)

    pl.loop(0, SPAN // 32)(forward_table)

    row = lax.broadcasted_iota(jnp.int32, (2 * BINS, 1), 0)
    row_quarter = jnp.where(row < BINS, 0.0, 0.25)
    row_place = jnp.where(row < BINS, row, row - BINS).astype(jnp.float32)
    c, s = cos_sin(row_place * (float_iota((1, INNER), 1) * (1.0 / INNER)) + row_quarter)
    for base in (0, 2 * BINS):
        inv[0, base : base + 2 * BINS, :] = c.astype(jnp.bfloat16)
        inv[1, base : base + 2 * BINS, :] = s.astype(jnp.bfloat16)

    env_lane = lax.broadcasted_iota(jnp.int32, (1, FB), 1)
    env_place = jnp.where(env_lane < HALF_FB, env_lane, env_lane - HALF_FB).astype(jnp.float32)
    for odd in range(2):
        freq = (2.0 * env_place + (1.0 if odd else 2.0)) * (1.0 / TIMES)
        base_c, base_s = cos_sin(float_iota((32, FB), 0) * freq)
        lead_c, lead_s = cos_sin(float_iota((FOLD // 32, FB), 0) * (freq * 32.0))
        shown = (env_lane >= HALF_FB) == bool(odd)
        base_c, base_s = jnp.where(shown, base_c, 0.0), jnp.where(shown, base_s, 0.0)
        for a in range(FOLD // 32):
            lc, ls = lead_c[a : a + 1], lead_s[a : a + 1]
            at = slice(odd * FOLD + a * 32, odd * FOLD + (a + 1) * 32)
            env[0, at, :] = (lc * base_c - ls * base_s).astype(jnp.bfloat16)
            env[1, at, :] = -(ls * base_c + lc * base_s).astype(jnp.bfloat16)

    hear(0)

    delays_in.wait()
    nodes_d[...] = (d_ref[...].astype(jnp.float32) * unit).T
    bins = env_bins(1)

    def phases(step):
        at = pl.ds(pl.multiple_of(step * node_rows, node_rows), node_rows)
        delay = nodes_d[at, :]
        for ch in range(chans):
            c, s = cos_sin(delay[:, ch : ch + 1] * bins)
            phase_c[ch, at, :] = c
            phase_s[ch, at, :] = s

    def more_phases(step):
        for k in range(UNROLL):
            phases(UNROLL * step + k)

    steps = n_chan // UNROLL
    pl.loop(0, steps // 2)(more_phases)
    hear(1)
    pl.loop(steps // 2, steps)(more_phases)
    hear(2)

    turns = env_bins(0)
    c, s = cos_sin(turns * (float_iota((1, TB), 1) * (DEC * unit)))
    for first, value in ((0, c), (FB, -s)):
        for piece, part in enumerate(split(value)):
            turn_tab[first : first + FB, piece * TB : (piece + 1) * TB] = part
    offsets_in.wait()
    for w in range(kept):
        shift = off_ref[w].astype(jnp.float32) * unit
        turn_row[w, :, :FB], turn_row[w, :, FB:] = cos_sin(bins * shift)

    pltpu.make_async_copy(own, own, x_in).wait()

    def residues(at):
        mine = own[at, :].astype(jnp.float32)
        theirs = other[at, :].astype(jnp.float32)
        a, b = [], []
        for q in range(RADIX // 2):
            cols = slice(q * SPAN, (q + 1) * SPAN)
            a.append(mine[:, cols] + theirs[:, cols])
            b.append(mine[:, cols] - theirs[:, cols])
        s02, d02, s13, d13 = a[0] + a[2], a[0] - a[2], a[1] + a[3], a[1] - a[3]
        t, u = (b[1] - b[3]) * root_half, (b[1] + b[3]) * root_half
        one = (b[0] + t, -(u + b[2]))
        three = (b[0] - t, b[2] - u)
        parts = [
            (s02 + s13, None), one, (d02, -d13), three,
            (s02 - s13, None), (three[0], -three[1]), (d02, d13), (one[0], -one[1]),
        ]
        stacked = []
        for r in ORDER:
            re, im = parts[r]
            if r == 0:
                zr, zi = re, jnp.zeros_like(re)
            else:
                c, s = fwd_c[r : r + 1, :], fwd_s[r : r + 1, :]
                if im is None:
                    zr, zi = re * c, -(re * s)
                else:
                    zr, zi = re * c + im * s, im * c - re * s
            stacked.append(jnp.concatenate([zr, zi], axis=1).astype(jnp.bfloat16))
        return stacked

    def energies(inner):
        turned = [None] * RADIX
        for i, r in enumerate(ORDER):
            re, im = inner[i * TILE : (i + 1) * TILE, :INNER], inner[i * TILE : (i + 1) * TILE, INNER:]
            if r:
                c, s = inv_c[r : r + 1, :], inv_s[r : r + 1, :]
                re, im = re * c - im * s, re * s + im * c
            turned[r] = (re, im)
        evens, odds = inverse_four(turned[0::2]), inverse_four(turned[1::2])
        same, cross = [], []
        for q in range(RADIX // 2):
            (er, ei), (fr, fi) = evens[q], odds[q]
            same.append((er * er + ei * ei) + (fr * fr + fi * fi))
            if q == 0:
                both = 2.0 * (er * fr + ei * fi)
            elif q == 1:
                both = (2.0 * root_half) * (er * (fr - fi) + ei * (fr + fi))
            elif q == 2:
                both = 2.0 * (ei * fr - er * fi)
            else:
                both = (2.0 * root_half) * (ei * (fr - fi) - er * (fr + fi))
            cross.append(both)
        total = jnp.sum((same[0] + same[1]) + (same[2] + same[3]), axis=1, keepdims=True)
        factor = 4.0 / (math.sqrt(SAMPLES) * (total * (4.0 / SAMPLES) + epsilon))
        return jnp.concatenate(same + cross, axis=1).astype(jnp.bfloat16), factor

    def envelope(g):
        tiles = rows // TILE
        stacked = []
        for h in range(tiles):
            stacked += residues(pl.ds(pl.multiple_of(g * rows + h * TILE, TILE), TILE))
        spectrum = jnp.dot(jnp.concatenate(stacked, axis=0), fwd[...], preferred_element_type=jnp.float32)
        tapered = []
        for i in range(tiles * RADIX):
            r = ORDER[i % RADIX]
            high, low = split(spectrum[i * TILE : (i + 1) * TILE] * gain[r : r + 1, :])
            tapered.append(jnp.concatenate([high, low], axis=1))
        inner = jnp.dot(
            jnp.concatenate(tapered, axis=0), jnp.concatenate([inv[0], inv[1]], axis=1),
            preferred_element_type=jnp.float32,
        )
        found = [energies(inner[h * RADIX * TILE : (h + 1) * RADIX * TILE]) for h in range(tiles)]
        spread = jnp.dot(
            jnp.concatenate([energy for energy, _ in found], axis=0),
            jnp.concatenate([env[0], env[1]], axis=1), preferred_element_type=jnp.float32,
        )
        for h in range(tiles):
            e_tab[g, h * TILE : (h + 1) * TILE, :] = spread[h * TILE : (h + 1) * TILE] * found[h][1]

    def outgoing(dest):
        return pltpu.make_async_remote_copy(
            src_ref=send_buf.at[dest],
            dst_ref=recv_buf.at[me],
            send_sem=send_sem,
            recv_sem=recv_sem.at[me],
            device_id={"chan": dest},
            device_id_type=MESH,
        )

    def send(dest):
        @pl.when(dest != me)
        def _():
            outgoing(dest).start()

    def stack_up(g, dest, sums):
        at = pl.ds(pl.multiple_of(dest * node_rows, node_rows), node_rows)
        for ch in range(group):
            pc = phase_c[g * group + ch, at, :]
            ps = phase_s[g * group + ch, at, :]
            for w in range(kept):
                r = kept * ch + w
                er, ei = e_tab[g, r : r + 1, :FB], e_tab[g, r : r + 1, FB:]
                sums[0][w] = sums[0][w] + (pc * er - ps * ei)
                sums[1][w] = sums[1][w] + (pc * ei + ps * er)
        return sums

    def pack(dest, sums):
        packed = jnp.concatenate([sums[p][w] for p in range(2) for w in range(kept)], axis=0)
        send_buf[dest] = packed.astype(jnp.bfloat16)

    acc[...] = jnp.zeros_like(acc)

    @pl.loop(0, CHUNKS)
    def _(g):
        arrived = other.at[pl.ds(pl.multiple_of(g * rows, rows), rows)]
        to_partner(arrived, arrived, g).wait_recv()
        envelope(g)
        for step in range(EARLY):
            sums = stack_up(g, step, [[acc[step, p * kept + w] for w in range(kept)] for p in range(2)])
            for p in range(2):
                for w in range(kept):
                    acc[step, p * kept + w] = sums[p][w]

            pack(step, sums)
            if step:
                @pl.when(g == CHUNKS - 1)
                def _():
                    if step == 1:
                        for r in range(3, rounds):
                            hear(r)
                    send(step - 1)

    @pl.loop(EARLY, n_chan)
    def _(step):
        sums = [[jnp.zeros((node_rows, FB), jnp.float32) for _ in range(kept)] for _ in range(2)]
        for g in range(CHUNKS):
            sums = stack_up(g, step, sums)
        pack(step, sums)
        send(step - 1)

    send(n_chan - 1)

    def incoming(source):
        return pltpu.make_async_remote_copy(
            src_ref=send_buf.at[source],
            dst_ref=recv_buf.at[source],
            send_sem=send_sem,
            recv_sem=recv_sem.at[source],
            device_id={"chan": source},
            device_id_type=MESH,
        )

    to_partner(other, other, 0).wait_send()
    pltpu.make_async_remote_copy(
        src_ref=send_buf.at[pl.ds(0, n_chan - 1)],
        dst_ref=recv_buf.at[pl.ds(0, n_chan - 1)],
        send_sem=send_sem,
        recv_sem=recv_sem.at[0],
        device_id={"chan": flip(me, 0)},
        device_id_type=MESH,
    ).wait_send()

    def add_one(step, stack):
        source = lax.rem(me + step, n_chan)
        incoming(source).wait_recv()
        return stack + recv_buf[source].astype(jnp.float32)

    stack = lax.fori_loop(1, n_chan, add_one, send_buf[me].astype(jnp.float32))

    turned = []
    for w in range(kept):
        c, s = turn_row[w, :, :FB], turn_row[w, :, FB:]
        re = stack[w * node_rows : (w + 1) * node_rows]
        im = stack[(kept + w) * node_rows : (kept + w + 1) * node_rows]
        turned.append(jnp.concatenate([re * c - im * s, re * s + im * c], axis=1))
    high, low = split(jnp.concatenate(turned, axis=0))
    bright = jnp.dot(
        jnp.concatenate([high, low], axis=0), turn_tab[...], preferred_element_type=jnp.float32
    )
    size = kept * node_rows
    bright = bright[:size, :TB] + (bright[:size, TB:] + bright[size:, :TB])
    scale = 1.0 / math.sqrt(FB * chans * n_chan)
    out_ref[...] = (bright * scale).reshape(kept, node_rows, TB)


def solution(mesh):
    n_chan = mesh.shape["chan"]

    def on_device(traces, delays, offsets):
        chans, windows, half = traces.shape
        nodes = delays.shape[0]
        kept = offsets.shape[0]
        node_rows = nodes // n_chan
        packed_rows = 2 * kept * node_rows
        hbm = pl.BlockSpec(memory_space=pltpu.HBM)
        return pl.pallas_call(
            functools.partial(kernel, n_chan),
            out_shape=jax.ShapeDtypeStruct((kept, node_rows, TB), jnp.float32),
            in_specs=[hbm] * 3,
            out_specs=pl.BlockSpec(memory_space=pltpu.VMEM),
            scratch_shapes=[
                pltpu.VMEM((chans, nodes), jnp.int32),
                pltpu.VMEM((chans * kept, half), jnp.bfloat16),
                pltpu.VMEM((chans * kept, half), jnp.bfloat16),
                pltpu.VMEM((2 * SPAN, 2 * BINS), jnp.bfloat16),
                pltpu.VMEM((2, 4 * BINS, INNER), jnp.bfloat16),
                pltpu.VMEM((2, TIMES, FB), jnp.bfloat16),
                pltpu.VMEM((RADIX, SPAN), jnp.float32),
                pltpu.VMEM((RADIX, SPAN), jnp.float32),
                pltpu.VMEM((RADIX, INNER), jnp.float32),
                pltpu.VMEM((RADIX, INNER), jnp.float32),
                pltpu.VMEM((RADIX, 2 * BINS), jnp.float32),
                pltpu.VMEM((chans, nodes, FB), jnp.float32),
                pltpu.VMEM((chans, nodes, FB), jnp.float32),
                pltpu.VMEM((nodes, chans), jnp.float32),
                pltpu.VMEM((2 * FB, 2 * TB), jnp.bfloat16),
                pltpu.VMEM((kept, 1, 2 * FB), jnp.float32),
                pltpu.VMEM((CHUNKS, kept * chans // CHUNKS, 2 * FB), jnp.float32),
                pltpu.VMEM((EARLY, 2 * kept, node_rows, FB), jnp.float32),
                pltpu.VMEM((n_chan, packed_rows, FB), jnp.bfloat16),
                pltpu.VMEM((n_chan, packed_rows, FB), jnp.bfloat16),
                pltpu.SMEM((kept,), jnp.int32),
                pltpu.SemaphoreType.DMA,
                pltpu.SemaphoreType.DMA,
                pltpu.SemaphoreType.DMA,
                pltpu.SemaphoreType.DMA,
                pltpu.SemaphoreType.DMA((CHUNKS,)),
                pltpu.SemaphoreType.DMA,
                pltpu.SemaphoreType.DMA((n_chan,)),
                pltpu.SemaphoreType.REGULAR((n_chan.bit_length() - 1,)),
            ],
            compiler_params=pltpu.CompilerParams(
                collective_id=0, has_side_effects=True, vmem_limit_bytes=16 * 1024 * 1024 + 8 * chans * nodes * FB
            ),
        )(*(pltpu.with_memory_space_constraint(a, pltpu.HBM) for a in (traces, delays.T, offsets)))

    placed = (P("chan", None, "tm"), P(None, "chan"), P("tm"))
    return jax.shard_map(
        on_device, mesh=mesh, in_specs=placed, out_specs=P("tm", "chan", None), check_vma=False
    )
```
